512 devices in a mesh: lon: 16 (over x, y), sec: 32 (over z, core).
Axes of the slice: x: 4, y: 4, z: 16, core: 2. Of those that a mesh axis runs over, the one named last changes fastest.
Arguments:
- moisture: float32 [16, 512, 4096], P(None, 'sec', 'lon'), may hold values from 0 to 2
- heat: float32 [16, 512, 4096], P(None, 'sec', 'lon'), may hold values from -6 to 6
- moist_cond: float32 [16, 512, 4096], P(None, 'sec', 'lon'), may hold values from 0.05 to 2
- heat_cond: float32 [16, 512, 4096], P(None, 'sec', 'lon'), may hold values from 0.1 to 3
- rain: float32 [512, 4096], P('sec', 'lon'), may hold values from 0.01 to 1
- surface_flux: float32 [512, 4096], P('sec', 'lon'), may hold values from -6 to 6
- cell_reach: int32 [512, 4096], P('sec', 'lon'), may hold values from 0 to 65535
- records: bfloat16 [16, 65536, 256], P('lon', 'sec'), may hold values from 0 to 2
- unit_hydro: bfloat16 [16, 65536, 256], P('lon', 'sec'), may hold values from 0.049804688 to 1
- down_basin: int32 [16, 65536], P('lon', 'sec'), may hold values from 0 to 16383
- basin_home: int32 [16, 16384], P('lon'), may hold values from 0 to 16383, as said below
- send_index: int32 [16, 32, 32, 128], P('lon', 'sec'), may hold values from 0 to 2047, as said below
- send_count: int32 [16, 32, 32], P('lon', 'sec'), may hold values from 0 to 128, as said below
Outputs:
- moist_out: float32 [16, 512, 4096], P(None, 'sec', 'lon')
- heat_out: float32 [16, 512, 4096], P(None, 'sec', 'lon')
- record_out: bfloat16 [16, 65536, 256], P('lon', 'sec')
- basin_inflow: float32 [16, 16384, 256], P('lon', 'sec')
The draws below stay inside these ranges and needn't reach their ends.
Inputs may be any that keep to these rules, and one draw needn't show every extreme that they name: `send_index`: within a longitude group, device s lists each of its 2048 reaches in exactly one used slot; a reach listed in block d drains into a basin whose basin_home lies in d * 512 to (d+1) * 512 - 1. Unused slots hold 0. `send_count`: in every group one owner receives 128 reaches from every device of sec; counts of owners 2 m and 2 m + 1 from one device add up to 128. `basin_home`: each group's row is a permutation.
All inputs are finite; a program needn't handle non-finite values.
Results may differ from the reference program's by a relative error of at most 0.009.
Values may be sent and summed in bfloat16 or wider, within the bound.
A program may use at most 64 MiB of HBM per device.

```python
import math
import jax
import jax.numpy as jnp
from jax import lax

NL = 16
LON_DEV = 256
H = 256
R_DEV = 2048
B_DEV = 512
CAP = 128
REACHES = 65536
BASINS = 16384
NLAT = 512
NLON = 4096
N_LON = 16
N_SEC = 32


def build_group(key):
    k_home, k_star, k_pairs, k_order, k_basin = jax.random.split(key, 5)
    inverse = jax.random.permutation(k_home, BASINS).astype(jnp.int32)
    homes = jnp.argsort(inverse, stable=True).astype(jnp.int32)
    star = jax.random.randint(k_star, (), 0, N_SEC, dtype=jnp.int32)
    pairs = jax.random.randint(k_pairs, (N_SEC, N_SEC // 2), 0, CAP + 1, dtype=jnp.int32)
    pair_ids = jnp.arange(N_SEC // 2, dtype=jnp.int32)
    forced = jnp.where(star % 2 == 0, CAP, 0).astype(jnp.int32)
    pairs = jnp.where(pair_ids[None, :] == star // 2, forced, pairs)
    counts = jnp.stack([pairs, CAP - pairs], axis=-1).reshape(N_SEC, N_SEC).astype(jnp.int32)
    ends = jnp.cumsum(counts, axis=1).astype(jnp.int32)
    starts = ends - counts
    order = jax.vmap(lambda k: jax.random.permutation(k, R_DEV).astype(jnp.int32))(jax.random.split(k_order, N_SEC))
    position = jnp.minimum(starts[:, :, None] + jnp.arange(CAP, dtype=jnp.int32)[None, None, :], R_DEV - 1)
    picked = jax.vmap(lambda line, place: line[place])(order, position)
    usable = jnp.arange(CAP, dtype=jnp.int32)[None, None, :] < counts[:, :, None]
    blocks = jnp.where(usable, picked, 0).astype(jnp.int32)
    owner = jnp.sum((ends[:, None, :] <= jnp.arange(R_DEV, dtype=jnp.int32)[None, :, None]).astype(jnp.int32), axis=-1)
    local_place = jax.random.randint(k_basin, (N_SEC, R_DEV), 0, B_DEV, dtype=jnp.int32)
    basin_at = inverse[owner * B_DEV + local_place]
    back = jnp.argsort(order, axis=1, stable=True)
    basins = jnp.take_along_axis(basin_at, back, axis=1).reshape(N_SEC * R_DEV).astype(jnp.int32)
    return (blocks, counts, basins, homes)


def build_all(key):
    base = jax.random.fold_in(key, 7)
    keys = jax.vmap(lambda g: jax.random.fold_in(base, g))(jnp.arange(N_LON))
    return jax.vmap(build_group)(keys)


def draw_send_index(key, part):
    return build_all(key)[0]


def draw_send_count(key, part):
    return build_all(key)[1]


def draw_down_basin(key, part):
    return build_all(key)[2]


def draw_basin_home(key, part):
    return build_all(key)[3]


def set_ends(entries, rng, low, high):
    shape = entries.shape
    index_at = [jax.random.randint(jax.random.fold_in(rng, axis), (), 0, shape[axis]) for axis in range(len(shape))]
    entries = entries.at[tuple(index_at)].set(low)
    longest = shape.index(max(shape))
    index_at[longest] = (index_at[longest] + 1) % shape[longest]
    return entries.at[tuple(index_at)].set(high)


def shard_levels(key, dims, pieces, least, top_value):
    gain = 1.0
    for axis_at, shards_of in pieces:
        heights = jax.random.uniform(jax.random.fold_in(jax.random.fold_in(key, 6), axis_at), (shards_of,), jnp.float32, least / len(pieces), top_value / len(pieces))
        gain = gain * jnp.repeat(jnp.exp(heights), dims[axis_at] // shards_of).reshape((-1,) + (1,) * (len(dims) - 1 - axis_at))
    return gain


def centred(stream_key, dims, width, bound, pieces=(), kind=jnp.bfloat16):
    gain = shard_levels(stream_key, dims, pieces, -0.22, 0.18) if pieces else 1.0
    array = jax.random.normal(stream_key, dims, jnp.float32) * width * gain
    return jnp.minimum(jnp.maximum(array, -bound), bound).astype(kind)


def setup_inputs(seed: int = 0) -> dict:
    splits = jax.random.split(jax.random.key(seed), 14)
    moisture = jnp.clip(2.0 * jax.random.uniform(splits[0], (NL, NLAT, NLON), jnp.float32) ** shard_levels(splits[0], (NL, NLAT, NLON), ((1, 32), (2, 16)), -0.2, 0.2), 0.0, 2.0)
    heat = centred(splits[1], (NL, NLAT, NLON), 1.0, 6.0, ((1, 32), (2, 16)), jnp.float32)
    moist_cond = jnp.clip(jnp.exp(math.log(2.0) - 3.6888794 * jax.random.uniform(splits[2], (NL, NLAT, NLON), jnp.float32) ** shard_levels(splits[2], (NL, NLAT, NLON), ((1, 32), (2, 16)), -0.2, 0.2)), 0.05, 2.0)
    heat_cond = jnp.clip(jnp.exp(math.log(3.0) - 3.4011974 * jax.random.uniform(splits[3], (NL, NLAT, NLON), jnp.float32) ** shard_levels(splits[3], (NL, NLAT, NLON), ((1, 32), (2, 16)), -0.2, 0.2)), 0.1, 3.0)
    rain = jnp.clip(jnp.exp(math.log(1.0) - 4.6051702 * jax.random.uniform(splits[4], (NLAT, NLON), jnp.float32) ** shard_levels(splits[4], (NLAT, NLON), ((0, 32), (1, 16)), -0.2, 0.2)), 0.01, 1.0)
    surface_flux = centred(splits[5], (NLAT, NLON), 1.0, 6.0, ((0, 32), (1, 16)), jnp.float32)
    cell_reach = set_ends(jax.random.randint(splits[6], (NLAT, NLON), 0, REACHES), jax.random.fold_in(splits[6], 1), 0, REACHES - 1).astype(jnp.int32)
    records = jnp.clip(2.0 * jax.random.uniform(splits[7], (N_LON, REACHES, H), jnp.float32) ** shard_levels(splits[7], (N_LON, REACHES, H), ((0, 16), (1, 32)), -0.2, 0.2), 0.0, 2.0).astype(jnp.bfloat16)
    unit_hydro = jnp.clip(jnp.exp(math.log(1.0) - 2.9996462 * jax.random.uniform(splits[8], (N_LON, REACHES, H), jnp.float32) ** shard_levels(splits[8], (N_LON, REACHES, H), ((0, 16), (1, 32)), -0.2, 0.2)), 0.049804688, 1.0).astype(jnp.bfloat16)
    down_basin = draw_down_basin(jax.random.fold_in(splits[13], 71), 0)
    basin_home = draw_basin_home(jax.random.fold_in(splits[13], 71), 0)
    send_index = draw_send_index(jax.random.fold_in(splits[13], 71), 0)
    send_count = draw_send_count(jax.random.fold_in(splits[13], 71), 0)
    return dict(moisture=moisture, heat=heat, moist_cond=moist_cond, heat_cond=heat_cond, rain=rain, surface_flux=surface_flux, cell_reach=cell_reach, records=records, unit_hydro=unit_hydro, down_basin=down_basin, basin_home=basin_home, send_index=send_index, send_count=send_count)


LATERAL = 0.2


def lateral(field):
    padded = jnp.pad(field, ((0, 0), (1, 1), (1, 1)))
    beside_all = padded[:, 2:, 1:-1] + padded[:, :-2, 1:-1] + padded[:, 1:-1, 2:] + padded[:, 1:-1, :-2]
    return field + LATERAL * (beside_all - 4.0 * field)


def column_solve(conduct, source):
    layer_count = conduct.shape[0]
    flat_zero = jnp.zeros_like(conduct[0])
    links = [0.5 * (conduct[layer] + conduct[layer + 1]) for layer in range(layer_count - 1)]
    above_link = links + [flat_zero]
    below_link = [flat_zero] + links
    prev_ratio = flat_zero
    prev_value = flat_zero
    ratio_list = []
    value_list = []
    for layer in range(layer_count):
        pivot_value = 1.0 + below_link[layer] + above_link[layer] + below_link[layer] * prev_ratio
        prev_ratio = -above_link[layer] / pivot_value
        prev_value = (source[layer] + below_link[layer] * prev_value) / pivot_value
        ratio_list.append(prev_ratio)
        value_list.append(prev_value)
    result = [None] * layer_count
    result[layer_count - 1] = value_list[layer_count - 1]
    for layer in range(layer_count - 2, -1, -1):
        result[layer] = value_list[layer] - ratio_list[layer] * result[layer + 1]
    return jnp.stack(result)


def reference(moisture, heat, moist_cond, heat_cond, rain, surface_flux, cell_reach, records, unit_hydro, down_basin, basin_home, send_index, send_count):
    moist_rhs = lateral(moisture).at[0].add(rain)
    heat_rhs = lateral(heat).at[0].add(surface_flux)
    moist_out = column_solve(moist_cond, moist_rhs)
    heat_out = column_solve(heat_cond, heat_rhs)
    runoff = jax.nn.softplus(moist_out[0] - 1.0) * jax.nn.sigmoid(heat_out[0]) + 0.5 * moist_cond[NL - 1] * moist_out[NL - 1]
    group_runoff = runoff.reshape(NLAT, N_LON, LON_DEV).transpose(1, 0, 2).reshape(N_LON, NLAT * LON_DEV)
    group_cells = cell_reach.reshape(NLAT, N_LON, LON_DEV).transpose(1, 0, 2).reshape(N_LON, NLAT * LON_DEV)
    reach_runoff = jax.vmap(lambda vals, where: jax.ops.segment_sum(vals, where, num_segments=REACHES))(group_runoff, group_cells)
    shifted = jnp.concatenate([records[:, :, 1:].astype(jnp.float32), jnp.zeros((N_LON, REACHES, 1), jnp.float32)], axis=2)
    record_out = (shifted + reach_runoff[:, :, None] * unit_hydro.astype(jnp.float32)).astype(jnp.bfloat16)

    def one_group(inputs):
        blocks, counts, basins, homes, group_records = inputs
        offsets = (jnp.arange(N_SEC, dtype=jnp.int32) * R_DEV)[:, None, None]
        reach_rows = (blocks + offsets).astype(jnp.int32)
        usable = jnp.arange(CAP, dtype=jnp.int32)[None, None, :] < counts[:, :, None]
        home_slot = homes[basins[reach_rows]]
        target = jnp.where(usable, home_slot, BASINS).astype(jnp.int32)
        values = group_records[reach_rows].astype(jnp.float32).reshape(N_SEC * N_SEC * CAP, H)
        summed = jax.ops.segment_sum(values, target.reshape(-1), num_segments=BASINS + 1)
        return summed[:BASINS]

    basin_inflow = lax.map(one_group, (send_index, send_count, down_basin, basin_home, record_out))
    return moist_out, heat_out, record_out, basin_inflow
```

```python
import jax
import jax.numpy as jnp
from jax import lax
from jax.sharding import PartitionSpec as P

LATERAL = 0.2
BF = jnp.bfloat16
F32 = jnp.float32


def extended(cells, sides, width):
    for axis, dim in sides:
        count = lax.axis_size(axis)
        ends = count - 1
        head = lax.slice_in_dim(cells, 0, width, axis=dim)
        tail = lax.slice_in_dim(cells, cells.shape[dim] - width, cells.shape[dim], axis=dim)
        cells = jnp.concatenate(
            [
                lax.ppermute(tail, axis, [(i, (i + 1) % count) for i in range(ends)]),
                cells,
                lax.ppermute(head, axis, [((i + 1) % count, i) for i in range(ends)]),
            ],
            axis=dim,
        )
    return cells


def column_solve(conduct, source):
    layer_count = conduct.shape[0]
    flat_zero = jnp.zeros_like(conduct[0])
    links = [0.5 * (conduct[layer] + conduct[layer + 1]) for layer in range(layer_count - 1)]
    above_link = links + [flat_zero]
    below_link = [flat_zero] + links
    prev_ratio = flat_zero
    prev_value = flat_zero
    ratio_list = []
    value_list = []
    for layer in range(layer_count):
        pivot_value = 1.0 + below_link[layer] + above_link[layer] + below_link[layer] * prev_ratio
        prev_ratio = -above_link[layer] / pivot_value
        prev_value = (source[layer] + below_link[layer] * prev_value) / pivot_value
        ratio_list.append(prev_ratio)
        value_list.append(prev_value)
    result = [None] * layer_count
    result[layer_count - 1] = value_list[layer_count - 1]
    for layer in range(layer_count - 2, -1, -1):
        result[layer] = value_list[layer] - ratio_list[layer] * result[layer + 1]
    return jnp.stack(result)


def marks(ids, count, axis):
    shape = (count, 1) if axis == 0 else (1, count)
    ids = ids[None, :] if axis == 0 else ids[:, None]
    return ids == jnp.arange(count, dtype=jnp.int32).reshape(shape)


def per_device(
    moisture,
    heat,
    moist_cond,
    heat_cond,
    rain,
    surface_flux,
    cell_reach,
    records,
    unit_hydro,
    down_basin,
    basin_home,
    send_index,
    send_count,
):
    sections = lax.axis_size("sec")
    reaches = records.shape[1]
    steps_count = records.shape[2]
    capacity = send_index.shape[3]
    chips = sections // 2
    basin_local = basin_home.shape[1] // sections
    pairs = send_index[0, 0].reshape(chips, 2, capacity)
    first = send_count[0, 0].reshape(chips, 2)[:, :1]
    place = jnp.arange(capacity, dtype=jnp.int32)[None, :]
    packed = jnp.where(place < first, pairs[:, 0], jnp.flip(pairs[:, 1], axis=1)).reshape(-1)
    table = basin_home[0] % (2 * basin_local)
    table = jnp.concatenate(
        [(table // 256).reshape(-1, 128), (table % 256).reshape(-1, 128)], axis=1
    ).astype(BF)
    basins = down_basin[0]
    rows = jnp.dot(
        marks(basins // 128, table.shape[0], 1).astype(BF), table, preferred_element_type=F32
    )
    at = marks(basins % 128, 128, 1)
    high = jnp.sum(jnp.where(at, rows[:, :128], 0.0), axis=1)
    low = jnp.sum(jnp.where(at, rows[:, 128:], 0.0), axis=1)
    pick = marks(packed, reaches, 1).astype(BF)
    slots = jnp.dot(pick, jnp.stack([high, low], axis=1).astype(BF), preferred_element_type=F32)
    slots = (slots[:, 0] * 256.0 + slots[:, 1]).astype(jnp.int32)
    ids_got = lax.all_to_all(
        slots.reshape(sections, -1), "sec", split_axis=0, concat_axis=0, tiled=True
    )
    stacked = jnp.stack([moisture, heat])
    padded = extended(stacked.astype(BF), (("lon", 3), ("sec", 2)), 1).astype(F32)
    beside_all = (
        padded[:, :, 2:, 1:-1]
        + padded[:, :, :-2, 1:-1]
        + padded[:, :, 1:-1, 2:]
        + padded[:, :, 1:-1, :-2]
    )
    middle = stacked + LATERAL * (beside_all - 4.0 * stacked)
    moist_rhs = middle[0].at[0].add(rain)
    heat_rhs = middle[1].at[0].add(surface_flux)
    moist_out = column_solve(moist_cond, moist_rhs)
    heat_out = column_solve(heat_cond, heat_rhs)
    layer_last = moist_cond.shape[0] - 1
    runoff = (
        jax.nn.softplus(moist_out[0] - 1.0) * jax.nn.sigmoid(heat_out[0])
        + 0.5 * moist_cond[layer_last] * moist_out[layer_last]
    ).reshape(-1)
    cells = cell_reach.reshape(-1)
    spread = jnp.where(marks(cells // 256, sections * reaches // 256, 0), runoff[None, :], 0.0)
    terms = jnp.dot(
        spread.astype(BF), marks(cells % 256, 256, 1).astype(BF), preferred_element_type=F32
    )
    terms = lax.all_to_all(
        terms.astype(BF).reshape(sections, -1, 256), "sec", split_axis=0, concat_axis=0, tiled=True
    )
    reach_runoff = jnp.sum(terms.astype(F32), axis=0).reshape(-1)
    shifted = jnp.concatenate(
        [records[0][:, 1:].astype(F32), jnp.zeros((reaches, 1), F32)], axis=1
    )
    record_new = (shifted + reach_runoff[:, None] * unit_hydro[0].astype(F32)).astype(BF)
    moved = jnp.dot(pick, record_new, preferred_element_type=F32).astype(BF)
    arrived = lax.all_to_all(
        moved.reshape(sections, -1, steps_count), "sec", split_axis=0, concat_axis=0, tiled=True
    ).reshape(-1, steps_count)
    onehot = marks(ids_got.reshape(-1), 2 * basin_local, 0).astype(BF)
    sums = jnp.dot(onehot, arrived, preferred_element_type=F32)
    core = lax.axis_index("sec") % 2
    halves = sums.reshape(2, basin_local, steps_count)
    mine = jnp.where(core == 0, halves[0], halves[1])
    other = jnp.where(core == 0, halves[1], halves[0])
    inflow = mine + lax.ppermute(other, "sec", [(i, i ^ 1) for i in range(sections)])
    return (moist_out, heat_out, record_new[None], inflow[None])
def solution(mesh):
    placed = (
        P(None, "sec", "lon"),
        P(None, "sec", "lon"),
        P(None, "sec", "lon"),
        P(None, "sec", "lon"),
        P("sec", "lon"),
        P("sec", "lon"),
        P("sec", "lon"),
        P("lon", "sec", None),
        P("lon", "sec", None),
        P("lon", "sec"),
        P("lon", None),
        P("lon", "sec", None, None),
        P("lon", "sec", None),
    )
    return jax.shard_map(
        per_device,
        mesh=mesh,
        in_specs=placed,
        out_specs=(
            P(None, "sec", "lon"),
            P(None, "sec", "lon"),
            P("lon", "sec", None),
            P("lon", "sec", None),
        ),
        check_vma=False,
    )
```

```python
import jax
import jax.numpy as jnp
from jax import lax
from jax.experimental import pallas as pl
from jax.experimental.pallas import tpu as pltpu
from jax.sharding import PartitionSpec as P

LATERAL = 0.2
BF = jnp.bfloat16
F32 = jnp.float32
I32 = jnp.int32
NT = (((1,), (1,)), ((), ()))


def iota(shape, axis):
    return lax.broadcasted_iota(I32, shape, axis)


def ones_where(mask):
    return jnp.where(mask, 1.0, 0.0).astype(BF)


def dot(a, b):
    return jnp.dot(a, b, preferred_element_type=F32)


def dot_nt(a, b):
    return lax.dot_general(a, b, NT, preferred_element_type=F32)


def column(block, lane):
    shape = block.shape
    return jnp.sum(jnp.where(iota(shape, 1) == lane, block, 0.0), axis=1, keepdims=True)


def kernel(
    moist,
    heat,
    moist_cond,
    heat_cond,
    rain,
    flux,
    cells,
    records,
    hydro,
    basins,
    homes,
    send_index,
    send_count,
    moist_out,
    heat_out,
    record_out,
    inflow,
    base,
    inv,
    back,
    ratio,
    row_out,
    row_in,
    col_out,
    col_in,
    cells_in,
    value_out,
    value_in,
    hi,
    lo,
    value,
    spread,
    marks,
    terms_out,
    terms_in,
    places,
    picks,
    slots,
    ids_out,
    ids_in,
    shifted,
    hydro_at,
    rows_out,
    rows_in,
    chosen,
    sums,
    sums_in,
    halo_send,
    halo_recv,
    pair_send,
    pair_recv,
    terms_send,
    terms_recv,
    ids_send,
    ids_recv,
    rows_send,
    rows_recv,
):
    layers, lats, width = moist.shape
    chips = rows_out.shape[0]
    cap = rows_out.shape[1]
    steps = rows_out.shape[2]
    reaches = records.shape[0]
    lon, sec = lax.axis_index("lon"), lax.axis_index("sec")
    n_lon, n_sec = lax.axis_size("lon"), lax.axis_size("sec")
    chip, core = sec // 2, sec % 2
    partner = chip * 2 + 1 - core
    up, down = (sec + n_sec - 1) % n_sec, (sec + 1) % n_sec
    left, right = (lon + n_lon - 1) % n_lon, (lon + 1) % n_lon

    def ahead(k):
        return chips // 2 + ((k + 1) // 2) * (2 * (k % 2) - 1)

    def target(k):
        return (chip + ahead(k)) % chips

    def copy(src, dst, send, recv, **where):
        return pltpu.make_async_remote_copy(
            src_ref=src, dst_ref=dst, send_sem=send, recv_sem=recv, device_id=where
        )

    barrier = pltpu.get_barrier_semaphore()

    def greet(k, _):
        pl.semaphore_signal(barrier, inc=1, device_id={"sec": target(k) * 2 + core})
        return 0

    lax.fori_loop(0, chips - 1, greet, 0)
    for peer in ({"sec": up}, {"sec": down}, {"lon": left}, {"lon": right}):
        pl.semaphore_signal(barrier, inc=1, device_id=peer)

    lane_e = iota((lats, 128), 1)
    first = jnp.zeros((lats, 128), F32)
    last = jnp.zeros((lats, 128), F32)
    for f, field in enumerate((moist, heat)):
        row_out[0, f] = field[:, 0, :].astype(BF)
        row_out[1, f] = field[:, lats - 1, :].astype(BF)
        for layer in range(layers):
            first = jnp.where(lane_e == f * layers + layer, field[layer, :, 0:1], first)
            last = jnp.where(
                lane_e == f * layers + layer, field[layer, :, width - 1 : width], last
            )
    col_out[0] = first
    col_out[1] = last

    row_at, lane_at = iota((lats, width), 0), iota((lats, width), 1)
    for f, (field, cond, extra) in enumerate(
        ((moist, moist_cond, rain), (heat, heat_cond, flux))
    ):
        for layer in range(layers):
            x = field[layer]
            near = (
                jnp.where(row_at == 0, 0.0, pltpu.roll(x, 1, 0))
                + jnp.where(row_at == lats - 1, 0.0, pltpu.roll(x, lats - 1, 0))
                + jnp.where(lane_at == 0, 0.0, pltpu.roll(x, 1, 1))
                + jnp.where(lane_at == width - 1, 0.0, pltpu.roll(x, width - 1, 1))
            )
            x = x + LATERAL * (near - 4.0 * x)
            base[f, layer] = x + extra[...] if layer == 0 else x
        prev = jnp.zeros((lats, width), F32)
        below = jnp.zeros((lats, width), F32)
        for layer in range(layers):
            if layer + 1 < layers:
                above = 0.5 * (cond[layer] + cond[layer + 1])
            else:
                above = jnp.zeros((lats, width), F32)
            part = 1.0 / (1.0 + below + above + below * prev)
            prev = -above * part
            inv[f, layer] = part
            back[f, layer] = below * part
            ratio[f, layer] = prev
            below = above

    def cell_marks(at, where):
        reach = where[...]
        rows = pl.ds(at, lats)
        hi[rows] = jnp.where(
            (reach // reaches) % 2 == core,
            (reach // (2 * reaches)) * (reaches // 256) + (reach // 256) % (reaches // 256),
            -1,
        )
        lo[rows] = reach % 256

        def mark(r, _):
            lanes = pl.ds(pl.multiple_of(r * width, width), width)
            marks[:, lanes] = ones_where(lo[pl.ds(r, 1), :] == iota((256, width), 0))
            return 0

        lax.fori_loop(at, at + lats, mark, 0)

    cell_marks(0, cells)

    eye = ones_where(iota((128, 128), 0) == iota((128, 128), 1))
    flip = ones_where(iota((128, 128), 0) + iota((128, 128), 1) == 127)
    basin = basins[...]
    basin_cols = dot_nt(
        eye, jnp.concatenate([basin // 128, basin % 128], axis=0).astype(F32).astype(BF)
    )
    home = homes[...] % (2 * inflow.shape[0])
    table = jnp.concatenate([home // 256, home % 256], axis=1).astype(F32).astype(BF)
    groups = reaches // 128

    def look(m, _):
        found = dot(ones_where(column(basin_cols, m).astype(I32) == iota((128, 128), 1)), table)
        at = column(basin_cols, groups + m).astype(I32) == iota((128, 128), 1)
        high = jnp.sum(jnp.where(at, found[:, :128], 0.0), axis=1, keepdims=True)
        low = jnp.sum(jnp.where(at, found[:, 128:], 0.0), axis=1, keepdims=True)
        lane = iota((128, 128), 1)
        places[pl.ds(pl.multiple_of(m * 128, 128), 128), :] = jnp.where(
            lane == 0, high, jnp.where(lane == 1, low, 0.0)
        ).astype(BF)
        return 0

    lax.fori_loop(0, groups, look, 0)

    even = send_index[pl.ds(0, chips, stride=2), :]
    odd = send_index[pl.ds(1, chips, stride=2), :]

    def halves(x):
        return jnp.concatenate([x // 256, x % 256], axis=0).astype(F32).astype(BF)

    pick_even = ones_where(
        iota((2 * chips, 2 * chips), 0) == 2 * (iota((2 * chips, 2 * chips), 1) % chips)
    )
    counts = dot(
        jnp.broadcast_to(send_count[...], (8, 2 * chips)).astype(F32).astype(BF), pick_even
    )
    picks[...] = jnp.where(
        iota((cap, 2 * chips), 0).astype(F32) < counts[0:1, :],
        dot_nt(eye, halves(even)),
        dot_nt(flip, halves(odd)),
    )

    pl.semaphore_wait(barrier, chips - 1 + 4)

    halo = [
        copy(row_out.at[0], row_in.at[1], halo_send.at[0], halo_recv.at[1], sec=up),
        copy(row_out.at[1], row_in.at[0], halo_send.at[1], halo_recv.at[0], sec=down),
        copy(col_out.at[0], col_in.at[1], halo_send.at[2], halo_recv.at[3], lon=left),
        copy(col_out.at[1], col_in.at[0], halo_send.at[3], halo_recv.at[2], lon=right),
    ]
    reach_pair = copy(cells, cells_in, pair_send.at[0], pair_recv.at[0], sec=partner)
    for one in halo:
        one.start()
    reach_pair.start()
    reach_pair.wait()
    cell_marks(lats, cells_in)
    for one in halo:
        one.wait()

    has_up = jnp.where(sec > 0, LATERAL, 0.0)
    has_down = jnp.where(sec < n_sec - 1, LATERAL, 0.0)
    has_left = jnp.where(lon > 0, LATERAL, 0.0)
    has_right = jnp.where(lon < n_lon - 1, LATERAL, 0.0)
    runoff = None
    surface = []
    for f, out in enumerate((moist_out, heat_out)):
        above_rows = row_in[0, f].astype(F32) * has_up
        below_rows = row_in[1, f].astype(F32) * has_down
        first = col_in[0] * has_left
        last = col_in[1] * has_right
        held = []
        prev = jnp.zeros((lats, width), F32)
        for layer in range(layers):
            lane = f * layers + layer
            source = (
                base[f, layer]
                + jnp.where(row_at == 0, above_rows[layer : layer + 1, :], 0.0)
                + jnp.where(row_at == lats - 1, below_rows[layer : layer + 1, :], 0.0)
                + jnp.where(lane_at == 0, first[:, lane : lane + 1], 0.0)
                + jnp.where(lane_at == width - 1, last[:, lane : lane + 1], 0.0)
            )
            prev = source * inv[f, layer] + back[f, layer] * prev
            held.append(prev)
        x = held[-1]
        out[layers - 1] = x
        if f == 0:
            runoff = 0.5 * moist_cond[layers - 1] * x
        for layer in range(layers - 2, -1, -1):
            x = held[layer] - ratio[f, layer] * x
            out[layer] = x
        surface.append(x)
    wet = surface[0] - 1.0
    softplus = jnp.maximum(wet, 0.0) + jnp.log1p(jnp.exp(-jnp.abs(wet)))
    runoff = softplus * jax.nn.sigmoid(surface[1]) + runoff
    value_out[...] = runoff.astype(BF)
    value_pair = copy(value_out, value_in, pair_send.at[1], pair_recv.at[1], sec=partner)
    value_pair.start()
    value[pl.ds(0, lats)] = runoff

    def spread_rows(r, _):
        lanes = pl.ds(pl.multiple_of(r * width, width), width)
        at = hi[pl.ds(r, 1), :] == iota((spread.shape[0], width), 0)
        spread[:, lanes] = jnp.where(at, value[pl.ds(r, 1), :], 0.0).astype(BF)
        return 0

    lax.fori_loop(0, lats, spread_rows, 0)
    half = lats * width
    terms = dot_nt(spread[:, :half], marks[:, :half])
    value_pair.wait()
    value[pl.ds(lats, lats)] = value_in[...].astype(F32)
    lax.fori_loop(lats, 2 * lats, spread_rows, 0)
    terms = terms + dot_nt(spread[:, half:], marks[:, half:])
    terms_out[...] = terms.astype(BF).reshape(terms_out.shape)

    def terms_copy(k):
        return copy(
            terms_out.at[target(k)],
            terms_in.at[k],
            terms_send.at[k],
            terms_recv.at[k],
            sec=target(k) * 2 + core,
        )

    def terms_start(k, _):
        terms_copy(k).start()
        return 0

    lax.fori_loop(0, chips - 1, terms_start, 0)
    terms_in[chips - 1] = terms_out[chip]

    lane_s = iota((cap, steps), 1)

    def pack(m, ids):
        at = column(picks[...], m) * 256.0 + column(picks[...], chips + m)
        pick = ones_where(at.astype(I32) == iota((cap, reaches), 1))
        place = dot(pick, places[...])
        hydro_at[m] = dot(pick, hydro[...])
        moved = pltpu.roll(dot(pick, records[...]), steps - 1, 1)
        shifted[m] = jnp.where(lane_s == steps - 1, 0.0, moved)
        place = column(place, 0) * 256.0 + column(place, 1)
        return jnp.where(iota((cap, 128), 1) == m, place, ids)

    ids = lax.fori_loop(0, chips, pack, jnp.zeros((cap, 128), F32))
    slots[...] = ids.T.astype(I32)

    def ids_copy(k):
        return copy(
            ids_out.at[target(k)],
            ids_in.at[k],
            ids_send.at[k],
            ids_recv.at[k],
            sec=target(k) * 2 + core,
        )

    def ids_fill(m, _):
        ids_out[m] = jnp.broadcast_to(slots[pl.ds(m, 1), :], (8, 128))
        return 0

    def ids_start(k, _):
        ids_copy(k).start()
        return 0

    lax.fori_loop(0, chips, ids_fill, 0)
    lax.fori_loop(0, chips - 1, ids_start, 0)
    ids_in[chips - 1] = ids_out[chip]

    def terms_wait(k, _):
        terms_copy(k).wait()
        return 0

    lax.fori_loop(0, chips - 1, terms_wait, 0)
    reach_runoff = terms_in[0].astype(F32)
    for k in range(1, chips):
        reach_runoff = reach_runoff + terms_in[k].astype(F32)
    coarse = reach_runoff.astype(BF)
    fine = (reach_runoff - coarse.astype(F32)).astype(BF)
    both = jnp.concatenate([coarse.astype(F32), fine.astype(F32)], axis=0).astype(BF)
    parts = both.shape[0]

    def make_rows(m):
        octet = column(picks[...], m).astype(I32)
        found = dot(ones_where(octet == iota((cap, parts), 1) % (parts // 2)), both)
        at = column(picks[...], chips + m).astype(I32) == iota((cap, 256), 1)
        scale = jnp.sum(jnp.where(at, found, 0.0), axis=1, keepdims=True)
        return (shifted[m] + scale * hydro_at[m]).astype(BF)

    def rows_copy(k):
        return copy(
            rows_out.at[k],
            rows_in.at[k],
            rows_send.at[k],
            rows_recv.at[k],
            sec=target(k) * 2 + core,
        )

    def rows_start(k, _):
        rows_out[k] = make_rows(target(k))
        rows_copy(k).start()
        return 0

    lax.fori_loop(0, chips - 1, rows_start, 0)
    rows_in[chips - 1] = make_rows(chip)

    diagonal = iota((256, 256), 0) == iota((256, 256), 1)
    lane_w = iota((256, steps), 1)
    for j in range(reaches // 256):
        scale = jnp.sum(
            jnp.where(diagonal, reach_runoff[j : j + 1, :], 0.0), axis=1, keepdims=True
        )
        rows = pl.ds(j * 256, 256)
        moved = pltpu.roll(records[rows, :].astype(F32), steps - 1, 1)
        moved = jnp.where(lane_w == steps - 1, 0.0, moved)
        record_out[rows, :] = (moved + scale * hydro[rows, :].astype(F32)).astype(BF)

    def ids_wait(k, _):
        ids_copy(k).wait()
        return 0

    lax.fori_loop(0, chips - 1, ids_wait, 0)

    def choose(i, _):
        got = jnp.concatenate([ids_in[2 * i][0:1, :], ids_in[2 * i + 1][0:1, :]], axis=1)
        chosen[i] = ones_where(got == iota((sums.shape[0], 2 * cap), 0))
        return 0

    lax.fori_loop(0, chips // 2, choose, 0)

    def gain(i):
        pair = rows_in[pl.ds(2 * i, 2)].reshape(2 * cap, steps)
        return dot(chosen[i], pair)

    rows_copy(0).wait()
    rows_copy(1).wait()
    sums[...] = gain(0)

    def add(i, _):
        rows_copy(2 * i).wait()
        rows_copy(2 * i + 1).wait()
        sums[...] += gain(i)
        return 0

    lax.fori_loop(1, chips // 2 - 1, add, 0)
    rows_copy(chips - 2).wait()
    sums[...] += gain(chips // 2 - 1)
    mine = inflow.shape[0]
    swap = copy(
        sums.at[pl.ds(pl.multiple_of((1 - core) * mine, mine), mine)],
        sums_in,
        pair_send.at[2],
        pair_recv.at[2],
        sec=partner,
    )
    swap.start()
    swap.wait()
    inflow[...] = sums[pl.ds(pl.multiple_of(core * mine, mine), mine), :] + sums_in[...]


def per_device(
    moisture,
    heat,
    moist_cond,
    heat_cond,
    rain,
    surface_flux,
    cell_reach,
    records,
    unit_hydro,
    down_basin,
    basin_home,
    send_index,
    send_count,
):
    sections = lax.axis_size("sec")
    chips = sections // 2
    layers, lats, width = moisture.shape
    reaches, steps = records.shape[1:]
    cap = send_index.shape[3]
    mine = basin_home.shape[1] // sections
    field = (2, layers, lats, width)
    octets = reaches // 256
    vmem = pltpu.VMEM
    sem = pltpu.SemaphoreType.DMA
    out = pl.pallas_call(
        kernel,
        out_shape=(
            jax.ShapeDtypeStruct(moisture.shape, F32),
            jax.ShapeDtypeStruct(heat.shape, F32),
            jax.ShapeDtypeStruct((reaches, steps), BF),
            jax.ShapeDtypeStruct((mine, steps), F32),
        ),
        in_specs=[pl.BlockSpec(memory_space=vmem)] * 13,
        out_specs=tuple([pl.BlockSpec(memory_space=vmem)] * 4),
        scratch_shapes=[
            vmem(field, F32),
            vmem(field, F32),
            vmem(field, F32),
            vmem(field, F32),
            vmem((2, 2, layers, width), BF),
            vmem((2, 2, layers, width), BF),
            vmem((2, lats, 128), F32),
            vmem((2, lats, 128), F32),
            vmem((lats, width), I32),
            vmem((lats, width), BF),
            vmem((lats, width), BF),
            vmem((2 * lats, width), I32),
            vmem((2 * lats, width), I32),
            vmem((2 * lats, width), F32),
            vmem((chips * octets, 2 * lats * width), BF),
            vmem((256, 2 * lats * width), BF),
            vmem((chips, octets, 256), BF),
            vmem((chips, octets, 256), BF),
            vmem((reaches, 128), BF),
            vmem((cap, 2 * chips), F32),
            vmem((128, cap), I32),
            vmem((chips, 8, 128), I32),
            vmem((chips, 8, 128), I32),
            vmem((chips, cap, steps), F32),
            vmem((chips, cap, steps), F32),
            vmem((chips, cap, steps), BF),
            vmem((chips, cap, steps), BF),
            vmem((chips // 2, 2 * mine, 2 * cap), BF),
            vmem((2 * mine, steps), F32),
            vmem((mine, steps), F32),
            sem((4,)),
            sem((4,)),
            sem((3,)),
            sem((3,)),
            sem((chips,)),
            sem((chips,)),
            sem((chips,)),
            sem((chips,)),
            sem((chips,)),
            sem((chips,)),
        ],
        compiler_params=pltpu.CompilerParams(
            collective_id=0, has_side_effects=True, vmem_limit_bytes=60 * 1024 * 1024
        ),
    )(
        moisture,
        heat,
        moist_cond,
        heat_cond,
        rain,
        surface_flux,
        cell_reach,
        records[0],
        unit_hydro[0],
        down_basin.reshape(reaches // 128, 128),
        basin_home.reshape(-1, 128),
        send_index[0, 0],
        send_count[0],
    )
    return out[0], out[1], out[2][None], out[3][None]


def solution(mesh):
    placed = (
        P(None, "sec", "lon"),
        P(None, "sec", "lon"),
        P(None, "sec", "lon"),
        P(None, "sec", "lon"),
        P("sec", "lon"),
        P("sec", "lon"),
        P("sec", "lon"),
        P("lon", "sec", None),
        P("lon", "sec", None),
        P("lon", "sec"),
        P("lon", None),
        P("lon", "sec", None, None),
        P("lon", "sec", None),
    )
    return jax.shard_map(
        per_device,
        mesh=mesh,
        in_specs=placed,
        out_specs=(
            P(None, "sec", "lon"),
            P(None, "sec", "lon"),
            P("lon", "sec", None),
            P("lon", "sec", None),
        ),
        check_vma=False,
    )
```

```python
import jax
import jax.numpy as jnp
from jax import lax
from jax.experimental import pallas as pl
from jax.experimental.pallas import tpu as pltpu
from jax.sharding import PartitionSpec as P

LATERAL = 0.2
BF = jnp.bfloat16
F32 = jnp.float32
I32 = jnp.int32
NT = (((1,), (1,)), ((), ()))


def iota(shape, axis):
    return lax.broadcasted_iota(I32, shape, axis)


def ones_where(mask):
    return jnp.where(mask, 1.0, 0.0).astype(BF)


def dot(a, b):
    return jnp.dot(a, b, preferred_element_type=F32)


def dot_nt(a, b):
    return lax.dot_general(a, b, NT, preferred_element_type=F32)


def column(block, lane):
    shape = block.shape
    return jnp.sum(jnp.where(iota(shape, 1) == lane, block, 0.0), axis=1, keepdims=True)


def kernel(*refs):
    hbm, outs, rest = refs[:13], refs[13:17], refs[17:]
    local, rest = rest[:13], rest[13:]
    moist_out, heat_out, record_out, inflow, rest = *rest[:4], rest[4:]
    moist, heat, moist_cond, heat_cond, rain, flux, cells = local[:7]
    records, hydro, basins, homes, send_index, send_count = local[7:]
    (
        base,
        inv,
        back,
        ratio,
        row_out,
        row_in,
        col_out,
        col_in,
        cells_in,
        value_out,
        value_in,
        hi,
        lo,
        value,
        spread,
        marks,
        terms_out,
        terms_in,
        places,
        pick_rows,
        picks,
        ids_out,
        ids_in,
        ids_near,
        pick,
        shifted,
        hydro_at,
        rows_out,
        rows_in,
        rows_near,
        chosen,
        chosen_near,
        load_sem,
        save_sem,
        halo_send,
        halo_recv,
        pair_send,
        pair_recv,
        terms_send,
        terms_recv,
        ids_send,
        ids_recv,
        rows_send,
        rows_recv,
        near_send,
        near_recv,
    ) = rest
    layers, lats, width = moist.shape
    chips = rows_out.shape[0]
    cap = rows_out.shape[1]
    steps = rows_out.shape[2]
    reaches = records.shape[0]
    lon, sec = lax.axis_index("lon"), lax.axis_index("sec")
    n_lon, n_sec = lax.axis_size("lon"), lax.axis_size("sec")
    chip, core = sec // 2, sec % 2
    partner = chip * 2 + 1 - core
    up, down = (sec + n_sec - 1) % n_sec, (sec + 1) % n_sec
    left, right = (lon + n_lon - 1) % n_lon, (lon + 1) % n_lon

    def ahead(k):
        return chips // 2 + ((k + 1) // 2) * (2 * (k % 2) - 1)

    def target(k):
        return (chip + ahead(k)) % chips

    def copy(src, dst, send, recv, **where):
        return pltpu.make_async_remote_copy(
            src_ref=src, dst_ref=dst, send_sem=send, recv_sem=recv, device_id=where
        )

    barrier = pltpu.get_barrier_semaphore()

    def greet(k, _):
        pl.semaphore_signal(barrier, inc=1, device_id={"sec": target(k) * 2 + core})
        return 0

    lax.fori_loop(0, chips - 1, greet, 0)
    for peer in ({"sec": up}, {"sec": down}, {"lon": left}, {"lon": right}):
        pl.semaphore_signal(barrier, inc=1, device_id=peer)

    loads = [
        pltpu.make_async_copy(src, dst, load_sem.at[i])
        for i, (src, dst) in enumerate(zip(hbm, local))
    ]
    for i in (0, 1, 2, 3, 4, 5, 6, 9, 10, 11, 12, 7, 8):
        loads[i].start()

    def save(i, src):
        return pltpu.make_async_copy(src, outs[i], save_sem.at[i])

    for i in range(7):
        loads[i].wait()

    lane_e = iota((lats, 128), 1)
    first = jnp.zeros((lats, 128), F32)
    last = jnp.zeros((lats, 128), F32)
    for f, field in enumerate((moist, heat)):
        row_out[0, f] = field[:, 0, :].astype(BF)
        row_out[1, f] = field[:, lats - 1, :].astype(BF)
        for layer in range(layers):
            first = jnp.where(lane_e == f * layers + layer, field[layer, :, 0:1], first)
            last = jnp.where(
                lane_e == f * layers + layer, field[layer, :, width - 1 : width], last
            )
    col_out[0] = first
    col_out[1] = last

    row_at, lane_at = iota((lats, width), 0), iota((lats, width), 1)
    for f, (field, cond, extra) in enumerate(
        ((moist, moist_cond, rain), (heat, heat_cond, flux))
    ):
        for layer in range(layers):
            x = field[layer]
            near = (
                jnp.where(row_at == 0, 0.0, pltpu.roll(x, 1, 0))
                + jnp.where(row_at == lats - 1, 0.0, pltpu.roll(x, lats - 1, 0))
                + jnp.where(lane_at == 0, 0.0, pltpu.roll(x, 1, 1))
                + jnp.where(lane_at == width - 1, 0.0, pltpu.roll(x, width - 1, 1))
            )
            x = x + LATERAL * (near - 4.0 * x)
            base[f, layer] = x + extra[...] if layer == 0 else x
        prev = jnp.zeros((lats, width), F32)
        below = jnp.zeros((lats, width), F32)
        for layer in range(layers):
            if layer + 1 < layers:
                above = 0.5 * (cond[layer] + cond[layer + 1])
            else:
                above = jnp.zeros((lats, width), F32)
            part = 1.0 / (1.0 + below + above + below * prev)
            prev = -above * part
            inv[f, layer] = part
            back[f, layer] = below * part
            ratio[f, layer] = prev
            below = above

    def cell_marks(at, where):
        reach = where[...]
        rows = pl.ds(at, lats)
        hi[rows] = jnp.where(
            (reach // reaches) % 2 == core,
            (reach // (2 * reaches)) * (reaches // 256) + (reach // 256) % (reaches // 256),
            -1,
        )
        lo[rows] = reach % 256

        def mark(r, _):
            lanes = pl.ds(pl.multiple_of(r * width, width), width)
            marks[:, lanes] = ones_where(lo[pl.ds(r, 1), :] == iota((256, width), 0))
            return 0

        lax.fori_loop(at, at + lats, mark, 0)

    cell_marks(0, cells)

    for i in range(9, 13):
        loads[i].wait()
    home = (homes[...] % (2 * inflow.shape[0])).astype(F32).T.astype(I32)
    table = jnp.concatenate([home // 256, home % 256], axis=0).astype(F32).astype(BF)
    groups = reaches // 128

    def look(m, _):
        basin = basins[pl.ds(m, 1), :]
        found = dot(table, ones_where(basin // 128 == iota((128, 128), 0)))
        at = basin % 128 == iota((128, 128), 0)
        high = jnp.sum(jnp.where(at, found[:128], 0.0), axis=0, keepdims=True)
        low = jnp.sum(jnp.where(at, found[128:], 0.0), axis=0, keepdims=True)
        places[pl.ds(m, 1), :] = high
        places[pl.ds(groups + m, 1), :] = low
        return 0

    lax.fori_loop(0, groups, look, 0)

    even = send_index[pl.ds(0, chips, stride=2), :]
    odd = send_index[pl.ds(1, chips, stride=2), :]
    flip = ones_where(iota((128, 128), 0) + iota((128, 128), 1) == 127)

    def halves(x):
        return jnp.concatenate([x // 128, x % 128], axis=0).astype(F32)

    pick_even = ones_where(
        iota((2 * chips, 2 * chips), 1) == 2 * (iota((2 * chips, 2 * chips), 0) % chips)
    )
    counts = dot_nt(
        pick_even, jnp.broadcast_to(send_count[...], (8, 2 * chips)).astype(F32).astype(BF)
    )
    pick_rows[pl.ds(0, 2 * chips)] = jnp.where(
        iota((2 * chips, cap), 1).astype(F32) < counts[:, 0:1],
        halves(even),
        dot(halves(odd).astype(BF), flip),
    )
    pick_rows[pl.ds(2 * chips, cap - 2 * chips)] = jnp.zeros((cap - 2 * chips, cap), F32)
    picks[...] = pick_rows[...].T
    place_cols = places[...].T.astype(BF)

    def ids_fill(m, _):
        group = pick_rows[pl.ds(m, 1), :].astype(I32)
        at = pick_rows[pl.ds(chips + m, 1), :].astype(I32) == iota((128, cap), 0)
        digit = iota((2 * groups, cap), 0)
        found = dot(
            place_cols,
            jnp.concatenate(
                [ones_where(digit == group), ones_where(digit == group + groups)], axis=1
            ),
        )
        high = jnp.sum(jnp.where(at, found[:, :cap], 0.0), axis=0, keepdims=True)
        low = jnp.sum(jnp.where(at, found[:, cap:], 0.0), axis=0, keepdims=True)
        ids_out[m] = (high * 256.0 + low).astype(I32)
        return 0

    lax.fori_loop(0, chips, ids_fill, 0)

    pl.semaphore_wait(barrier, chips - 1 + 4)

    halo = [
        copy(row_out.at[0], row_in.at[1], halo_send.at[0], halo_recv.at[1], sec=up),
        copy(row_out.at[1], row_in.at[0], halo_send.at[1], halo_recv.at[0], sec=down),
        copy(col_out.at[0], col_in.at[1], halo_send.at[2], halo_recv.at[3], lon=left),
        copy(col_out.at[1], col_in.at[0], halo_send.at[3], halo_recv.at[2], lon=right),
    ]
    reach_pair = copy(cells, cells_in, pair_send.at[0], pair_recv.at[0], sec=partner)
    for one in halo:
        one.start()
    def ids_copy(k):
        return copy(
            ids_out.at[target(k)],
            ids_in.at[k],
            ids_send.at[k],
            ids_recv.at[k],
            sec=target(k) * 2 + core,
        )

    def ids_start(k, _):
        ids_copy(k).start()
        return 0

    reach_pair.start()
    lax.fori_loop(0, chips - 1, ids_start, 0)
    ids_in[chips - 1] = ids_out[chip]
    reach_pair.wait()
    cell_marks(lats, cells_in)
    for one in halo:
        one.wait()

    has_up = jnp.where(sec > 0, LATERAL, 0.0)
    has_down = jnp.where(sec < n_sec - 1, LATERAL, 0.0)
    has_left = jnp.where(lon > 0, LATERAL, 0.0)
    has_right = jnp.where(lon < n_lon - 1, LATERAL, 0.0)
    runoff = None
    surface = []
    for f, out in enumerate((moist_out, heat_out)):
        above_rows = row_in[0, f].astype(F32) * has_up
        below_rows = row_in[1, f].astype(F32) * has_down
        first = col_in[0] * has_left
        last = col_in[1] * has_right
        held = []
        prev = jnp.zeros((lats, width), F32)
        for layer in range(layers):
            lane = f * layers + layer
            source = (
                base[f, layer]
                + jnp.where(row_at == 0, above_rows[layer : layer + 1, :], 0.0)
                + jnp.where(row_at == lats - 1, below_rows[layer : layer + 1, :], 0.0)
                + jnp.where(lane_at == 0, first[:, lane : lane + 1], 0.0)
                + jnp.where(lane_at == width - 1, last[:, lane : lane + 1], 0.0)
            )
            prev = source * inv[f, layer] + back[f, layer] * prev
            held.append(prev)
        x = held[-1]
        out[pl.ds((layers - 1) * lats, lats), :] = x
        if f == 0:
            runoff = 0.5 * moist_cond[layers - 1] * x
        for layer in range(layers - 2, -1, -1):
            x = held[layer] - ratio[f, layer] * x
            out[pl.ds(layer * lats, lats), :] = x
        surface.append(x)
    wet = surface[0] - 1.0
    softplus = jnp.maximum(wet, 0.0) + jnp.log1p(jnp.exp(-jnp.abs(wet)))
    runoff = softplus * jax.nn.sigmoid(surface[1]) + runoff
    value_out[...] = runoff.astype(BF)
    value_pair = copy(value_out, value_in, pair_send.at[1], pair_recv.at[1], sec=partner)
    value_pair.start()
    value[pl.ds(0, lats)] = runoff

    def spread_rows(r, _):
        lanes = pl.ds(pl.multiple_of(r * width, width), width)
        at = hi[pl.ds(r, 1), :] == iota((spread.shape[0], width), 0)
        spread[:, lanes] = jnp.where(at, value[pl.ds(r, 1), :], 0.0).astype(BF)
        return 0

    lax.fori_loop(0, lats, spread_rows, 0)
    half = lats * width
    terms = dot_nt(spread[:, :half], marks[:, :half])
    value_pair.wait()
    value[pl.ds(lats, lats)] = value_in[...].astype(F32)
    lax.fori_loop(lats, 2 * lats, spread_rows, 0)
    terms = terms + dot_nt(spread[:, half:], marks[:, half:])
    terms_out[...] = terms.astype(BF).reshape(terms_out.shape)

    def terms_copy(k):
        return copy(
            terms_out.at[target(k)],
            terms_in.at[k],
            terms_send.at[k],
            terms_recv.at[k],
            sec=target(k) * 2 + core,
        )

    def terms_start(k, _):
        terms_copy(k).start()
        return 0

    lax.fori_loop(0, chips - 1, terms_start, 0)
    save(0, moist_out).start()
    save(1, heat_out).start()
    terms_in[chips - 1] = terms_out[chip]

    loads[7].wait()
    loads[8].wait()
    lane_s = iota((cap, steps), 1)
    batch = pick.shape[0] // cap

    def pack(i, _):
        for b in range(batch):
            at = column(picks[...], i * batch + b) * 128.0
            at = at + column(picks[...], chips + i * batch + b)
            pick[pl.ds(b * cap, cap), :] = ones_where(at.astype(I32) == iota((cap, reaches), 1))
        now = pl.ds(i * batch, batch)
        hydro_at[now] = dot(pick[...], hydro[...]).reshape(batch, cap, steps)
        moved = dot(pick[...], records[...])
        for b in range(batch):
            one = pltpu.roll(moved[b * cap : (b + 1) * cap], steps - 1, 1)
            shifted[i * batch + b] = jnp.where(lane_s == steps - 1, 0.0, one)
        return 0

    lax.fori_loop(0, chips // batch, pack, 0)

    def ids_wait(k, _):
        ids_copy(k).wait()
        return 0

    lax.fori_loop(0, chips - 1, ids_wait, 0)
    ids_pair = copy(ids_in, ids_near, pair_send.at[2], pair_recv.at[2], sec=partner)
    ids_pair.start()

    def terms_wait(k, _):
        terms_copy(k).wait()
        return 0

    lax.fori_loop(0, chips - 1, terms_wait, 0)
    reach_runoff = terms_in[0].astype(F32)
    for k in range(1, chips):
        reach_runoff = reach_runoff + terms_in[k].astype(F32)
    coarse = reach_runoff.astype(BF)
    fine = (reach_runoff - coarse.astype(F32)).astype(BF)
    both = jnp.concatenate([coarse.astype(F32), fine.astype(F32)], axis=0).astype(BF)
    parts = both.shape[0]

    def make_rows(m):
        index = column(picks[...], m) * 128.0 + column(picks[...], chips + m)
        octet = index.astype(I32) // 256
        found = dot(ones_where(octet == iota((cap, parts), 1) % (parts // 2)), both)
        at = index.astype(I32) % 256 == iota((cap, 256), 1)
        scale = jnp.sum(jnp.where(at, found, 0.0), axis=1, keepdims=True)
        return (shifted[m] + scale * hydro_at[m]).astype(BF)

    def rows_copy(k):
        return copy(
            rows_out.at[k],
            rows_in.at[k],
            rows_send.at[k],
            rows_recv.at[k],
            sec=target(k) * 2 + core,
        )

    def rows_start(k, _):
        rows_out[k] = make_rows(target(k))
        rows_copy(k).start()
        return 0

    lax.fori_loop(0, chips - 1, rows_start, 0)
    rows_in[chips - 1] = make_rows(chip)

    diagonal = iota((256, 256), 0) == iota((256, 256), 1)
    lane_w = iota((256, steps), 1)
    for j in range(reaches // 256):
        scale = jnp.sum(
            jnp.where(diagonal, reach_runoff[j : j + 1, :], 0.0), axis=1, keepdims=True
        )
        rows = pl.ds(j * 256, 256)
        moved = pltpu.roll(records[rows, :].astype(F32), steps - 1, 1)
        moved = jnp.where(lane_w == steps - 1, 0.0, moved)
        record_out[rows, :] = (moved + scale * hydro[rows, :].astype(F32)).astype(BF)

    save(2, record_out).start()
    ids_pair.wait()
    mine = inflow.shape[0]
    basin_at = iota((mine, 2 * cap), 0) + core * mine

    def choose(i, _):
        for marked, ids in ((chosen, ids_in), (chosen_near, ids_near)):
            got = jnp.concatenate([ids[2 * i], ids[2 * i + 1]], axis=1)
            marked[i] = ones_where(got == basin_at)
        return 0

    lax.fori_loop(0, chips // 2, choose, 0)

    def gain(i, marked, rows):
        return dot(marked[i], rows[pl.ds(2 * i, 2)].reshape(2 * cap, steps))

    def near_copy(i):
        pair = pl.ds(2 * i, 2)
        return copy(
            rows_in.at[pair], rows_near.at[pair], near_send.at[i], near_recv.at[i], sec=partner
        )

    last = chips // 2 - 1
    rows_copy(0).wait()
    rows_copy(1).wait()
    near_copy(0).start()
    inflow[...] = gain(0, chosen, rows_in)

    def add(i, _):
        rows_copy(2 * i).wait()
        rows_copy(2 * i + 1).wait()
        near_copy(i).start()
        near_copy(i - 1).wait()
        inflow[...] += gain(i, chosen, rows_in) + gain(i - 1, chosen_near, rows_near)
        return 0

    lax.fori_loop(1, last, add, 0)
    rows_copy(chips - 2).wait()
    near_copy(last).start()
    near_copy(last - 1).wait()
    inflow[...] += gain(last, chosen, rows_in) + gain(last - 1, chosen_near, rows_near)
    near_copy(last).wait()
    inflow[...] += gain(last, chosen_near, rows_near)
    save(3, inflow).start()
    for i, done in enumerate((moist_out, heat_out, record_out, inflow)):
        save(i, done).wait()


def hand_over(*refs):
    srcs, dsts, held, load_sem, save_sem = refs[:4], refs[4:8], refs[8:12], refs[12], refs[13]
    order = (2, 3, 0, 1)
    loads = [pltpu.make_async_copy(srcs[i], held[i], load_sem.at[i]) for i in range(4)]
    saves = [pltpu.make_async_copy(held[i], dsts[i], save_sem.at[i]) for i in range(4)]
    for i in order:
        loads[i].start()
    for i in order:
        loads[i].wait()
        saves[i].start()
    for i in order:
        saves[i].wait()


def per_device(
    moisture,
    heat,
    moist_cond,
    heat_cond,
    rain,
    surface_flux,
    cell_reach,
    records,
    unit_hydro,
    down_basin,
    basin_home,
    send_index,
    send_count,
):
    sections = lax.axis_size("sec")
    chips = sections // 2
    layers, lats, width = moisture.shape
    reaches, steps = records.shape[1:]
    cap = send_index.shape[3]
    mine = basin_home.shape[1] // sections
    field = (2, layers, lats, width)
    octets = reaches // 256
    vmem = pltpu.VMEM
    sem = pltpu.SemaphoreType.DMA
    args = (
        moisture,
        heat,
        moist_cond,
        heat_cond,
        rain,
        surface_flux,
        cell_reach,
        records[0],
        unit_hydro[0],
        down_basin.reshape(reaches // 128, 128),
        basin_home.reshape(-1, 128),
        send_index[0, 0],
        send_count[0],
    )
    results = (
        jax.ShapeDtypeStruct((layers * lats, width), F32),
        jax.ShapeDtypeStruct((layers * lats, width), F32),
        jax.ShapeDtypeStruct((reaches, steps), BF),
        jax.ShapeDtypeStruct((mine, steps), F32),
    )
    anywhere = pl.BlockSpec(memory_space=pl.ANY)
    out = pl.pallas_call(
        kernel,
        out_shape=results,
        in_specs=[anywhere] * 13,
        out_specs=(anywhere,) * 4,
        scratch_shapes=[vmem(a.shape, a.dtype) for a in args + results]
        + [
            vmem(field, F32),
            vmem(field, F32),
            vmem(field, F32),
            vmem(field, F32),
            vmem((2, 2, layers, width), BF),
            vmem((2, 2, layers, width), BF),
            vmem((2, lats, 128), F32),
            vmem((2, lats, 128), F32),
            vmem((lats, width), I32),
            vmem((lats, width), BF),
            vmem((lats, width), BF),
            vmem((2 * lats, width), I32),
            vmem((2 * lats, width), I32),
            vmem((2 * lats, width), F32),
            vmem((chips * octets, 2 * lats * width), BF),
            vmem((256, 2 * lats * width), BF),
            vmem((chips, octets, 256), BF),
            vmem((chips, octets, 256), BF),
            vmem((2 * reaches // 128, 128), F32),
            vmem((cap, cap), F32),
            vmem((cap, cap), F32),
            vmem((chips, 1, cap), I32),
            vmem((chips, 1, cap), I32),
            vmem((chips, 1, cap), I32),
            vmem((4 * cap, reaches), BF),
            vmem((chips, cap, steps), F32),
            vmem((chips, cap, steps), F32),
            vmem((chips, cap, steps), BF),
            vmem((chips, cap, steps), BF),
            vmem((chips, cap, steps), BF),
            vmem((chips // 2, mine, 2 * cap), BF),
            vmem((chips // 2, mine, 2 * cap), BF),
            sem((13,)),
            sem((4,)),
            sem((4,)),
            sem((4,)),
            sem((3,)),
            sem((3,)),
            sem((chips,)),
            sem((chips,)),
            sem((chips,)),
            sem((chips,)),
            sem((chips,)),
            sem((chips,)),
            sem((chips // 2,)),
            sem((chips // 2,)),
        ],
        compiler_params=pltpu.CompilerParams(
            collective_id=0, has_side_effects=True, vmem_limit_bytes=60 * 1024 * 1024
        ),
    )(*args)
    out = pl.pallas_call(
        hand_over,
        out_shape=results,
        in_specs=[anywhere] * 4,
        out_specs=(anywhere,) * 4,
        scratch_shapes=[vmem(a.shape, a.dtype) for a in results] + [sem((4,)), sem((4,))],
    )(*out)
    fields = (layers, lats, width)
    return out[0].reshape(fields), out[1].reshape(fields), out[2][None], out[3][None]


def solution(mesh):
    placed = (
        P(None, "sec", "lon"),
        P(None, "sec", "lon"),
        P(None, "sec", "lon"),
        P(None, "sec", "lon"),
        P("sec", "lon"),
        P("sec", "lon"),
        P("sec", "lon"),
        P("lon", "sec", None),
        P("lon", "sec", None),
        P("lon", "sec"),
        P("lon", None),
        P("lon", "sec", None, None),
        P("lon", "sec", None),
    )
    return jax.shard_map(
        per_device,
        mesh=mesh,
        in_specs=placed,
        out_specs=(
            P(None, "sec", "lon"),
            P(None, "sec", "lon"),
            P("lon", "sec", None),
            P("lon", "sec", None),
        ),
        check_vma=False,
    )
```

```python
import jax
import jax.numpy as jnp
from jax import lax
from jax.experimental import pallas as pl
from jax.experimental.pallas import tpu as pltpu
from jax.sharding import PartitionSpec as P

LATERAL = 0.2
BF = jnp.bfloat16
F32 = jnp.float32
I32 = jnp.int32
NT = (((1,), (1,)), ((), ()))


def iota(shape, axis):
    return lax.broadcasted_iota(I32, shape, axis)


def ones_where(mask):
    return jnp.where(mask, 1.0, 0.0).astype(BF)


def dot(a, b):
    return jnp.dot(a, b, preferred_element_type=F32)


def dot_nt(a, b):
    return lax.dot_general(a, b, NT, preferred_element_type=F32)


def column(block, lane):
    shape = block.shape
    return jnp.sum(jnp.where(iota(shape, 1) == lane, block, 0.0), axis=1, keepdims=True)


def kernel(*refs):
    hbm, outs, rest = refs[:13], refs[13:17], refs[17:]
    local, rest = rest[:13], rest[13:]
    moist_out, heat_out, record_out, inflow, rest = *rest[:4], rest[4:]
    moist, heat, moist_cond, heat_cond, rain, flux, cells = local[:7]
    records, hydro, basins, homes, send_index, send_count = local[7:]
    (
        base,
        inv,
        back,
        ratio,
        row_out,
        row_in,
        col_out,
        col_in,
        cells_in,
        value_out,
        value_in,
        hi,
        lo,
        value,
        spread,
        marks,
        terms_out,
        terms_in,
        places,
        pick_rows,
        picks,
        ids_out,
        ids_in,
        ids_near,
        pick,
        shifted,
        hydro_at,
        rows_out,
        rows_in,
        rows_near,
        chosen,
        chosen_near,
        load_sem,
        save_sem,
        halo_send,
        halo_recv,
        pair_send,
        pair_recv,
        terms_send,
        terms_recv,
        ids_send,
        ids_recv,
        rows_send,
        rows_recv,
        near_send,
        near_recv,
    ) = rest
    layers, lats, width = moist.shape
    chips = rows_out.shape[0]
    cap = rows_out.shape[1]
    steps = rows_out.shape[2]
    reaches = records.shape[0]
    lon, sec = lax.axis_index("lon"), lax.axis_index("sec")
    n_lon, n_sec = lax.axis_size("lon"), lax.axis_size("sec")
    chip, core = sec // 2, sec % 2
    partner = chip * 2 + 1 - core
    up, down = (sec + n_sec - 1) % n_sec, (sec + 1) % n_sec
    left, right = (lon + n_lon - 1) % n_lon, (lon + 1) % n_lon

    def ahead(k):
        return chips // 2 + ((k + 1) // 2) * (2 * (k % 2) - 1)

    def target(k):
        return (chip + ahead(k)) % chips

    def copy(src, dst, send, recv, **where):
        return pltpu.make_async_remote_copy(
            src_ref=src, dst_ref=dst, send_sem=send, recv_sem=recv, device_id=where
        )

    barrier = pltpu.get_barrier_semaphore()

    def greet(k, _):
        pl.semaphore_signal(barrier, inc=1, device_id={"sec": target(k) * 2 + core})
        return 0

    lax.fori_loop(0, chips - 1, greet, 0)
    for peer in ({"sec": up}, {"sec": down}, {"lon": left}, {"lon": right}):
        pl.semaphore_signal(barrier, inc=1, device_id=peer)

    loads = [
        pltpu.make_async_copy(src, dst, load_sem.at[i])
        for i, (src, dst) in enumerate(zip(hbm, local))
    ]
    for i in (0, 1, 2, 3, 4, 5, 6, 9, 10, 11, 12, 7, 8):
        loads[i].start()

    def save(i, src):
        return pltpu.make_async_copy(src, outs[i], save_sem.at[i])

    for i in range(7):
        loads[i].wait()

    lane_e = iota((lats, 128), 1)
    first = jnp.zeros((lats, 128), F32)
    last = jnp.zeros((lats, 128), F32)
    for f, field in enumerate((moist, heat)):
        row_out[0, f] = field[:, 0, :].astype(BF)
        row_out[1, f] = field[:, lats - 1, :].astype(BF)
        for layer in range(layers):
            first = jnp.where(lane_e == f * layers + layer, field[layer, :, 0:1], first)
            last = jnp.where(
                lane_e == f * layers + layer, field[layer, :, width - 1 : width], last
            )
    col_out[0] = first
    col_out[1] = last

    row_at, lane_at = iota((lats, width), 0), iota((lats, width), 1)
    for f, (field, cond, extra) in enumerate(
        ((moist, moist_cond, rain), (heat, heat_cond, flux))
    ):
        for layer in range(layers):
            x = field[layer]
            near = (
                jnp.where(row_at == 0, 0.0, pltpu.roll(x, 1, 0))
                + jnp.where(row_at == lats - 1, 0.0, pltpu.roll(x, lats - 1, 0))
                + jnp.where(lane_at == 0, 0.0, pltpu.roll(x, 1, 1))
                + jnp.where(lane_at == width - 1, 0.0, pltpu.roll(x, width - 1, 1))
            )
            x = x + LATERAL * (near - 4.0 * x)
            base[f, layer] = x + extra[...] if layer == 0 else x
        prev = jnp.zeros((lats, width), F32)
        below = jnp.zeros((lats, width), F32)
        for layer in range(layers):
            if layer + 1 < layers:
                above = 0.5 * (cond[layer] + cond[layer + 1])
            else:
                above = jnp.zeros((lats, width), F32)
            part = 1.0 / (1.0 + below + above + below * prev)
            prev = -above * part
            inv[f, layer] = part
            back[f, layer] = below * part
            ratio[f, layer] = prev
            below = above

    def cell_marks(at, where):
        reach = where[...]
        rows = pl.ds(at, lats)
        hi[rows] = jnp.where(
            (reach // reaches) % 2 == core,
            (reach // (2 * reaches)) * (reaches // 256) + (reach // 256) % (reaches // 256),
            -1,
        )
        lo[rows] = reach % 256

        def mark(r, _):
            lanes = pl.ds(pl.multiple_of(r * width, width), width)
            marks[:, lanes] = ones_where(lo[pl.ds(r, 1), :] == iota((256, width), 0))
            return 0

        lax.fori_loop(at, at + lats, mark, 0)

    pl.semaphore_wait(barrier, chips - 1 + 4)

    halo = [
        copy(row_out.at[0], row_in.at[1], halo_send.at[0], halo_recv.at[1], sec=up),
        copy(row_out.at[1], row_in.at[0], halo_send.at[1], halo_recv.at[0], sec=down),
        copy(col_out.at[0], col_in.at[1], halo_send.at[2], halo_recv.at[3], lon=left),
        copy(col_out.at[1], col_in.at[0], halo_send.at[3], halo_recv.at[2], lon=right),
    ]
    reach_pair = copy(cells, cells_in, pair_send.at[0], pair_recv.at[0], sec=partner)
    for one in halo:
        one.start()
    reach_pair.start()
    cell_marks(0, cells)
    reach_pair.wait()
    cell_marks(lats, cells_in)
    for one in halo:
        one.wait()

    has_up = jnp.where(sec > 0, LATERAL, 0.0)
    has_down = jnp.where(sec < n_sec - 1, LATERAL, 0.0)
    has_left = jnp.where(lon > 0, LATERAL, 0.0)
    has_right = jnp.where(lon < n_lon - 1, LATERAL, 0.0)
    runoff = None
    surface = []
    for f, out in enumerate((moist_out, heat_out)):
        above_rows = row_in[0, f].astype(F32) * has_up
        below_rows = row_in[1, f].astype(F32) * has_down
        first = col_in[0] * has_left
        last = col_in[1] * has_right
        held = []
        prev = jnp.zeros((lats, width), F32)
        for layer in range(layers):
            lane = f * layers + layer
            source = (
                base[f, layer]
                + jnp.where(row_at == 0, above_rows[layer : layer + 1, :], 0.0)
                + jnp.where(row_at == lats - 1, below_rows[layer : layer + 1, :], 0.0)
                + jnp.where(lane_at == 0, first[:, lane : lane + 1], 0.0)
                + jnp.where(lane_at == width - 1, last[:, lane : lane + 1], 0.0)
            )
            prev = source * inv[f, layer] + back[f, layer] * prev
            held.append(prev)
        x = held[-1]
        out[pl.ds((layers - 1) * lats, lats), :] = x
        if f == 0:
            runoff = 0.5 * moist_cond[layers - 1] * x
        for layer in range(layers - 2, -1, -1):
            x = held[layer] - ratio[f, layer] * x
            out[pl.ds(layer * lats, lats), :] = x
        surface.append(x)
    wet = surface[0] - 1.0
    softplus = jnp.maximum(wet, 0.0) + jnp.log1p(jnp.exp(-jnp.abs(wet)))
    runoff = softplus * jax.nn.sigmoid(surface[1]) + runoff
    value_out[...] = runoff.astype(BF)
    value_pair = copy(value_out, value_in, pair_send.at[1], pair_recv.at[1], sec=partner)
    value_pair.start()
    value[pl.ds(0, lats)] = runoff

    def spread_rows(r, _):
        lanes = pl.ds(pl.multiple_of(r * width, width), width)
        at = hi[pl.ds(r, 1), :] == iota((spread.shape[0], width), 0)
        spread[:, lanes] = jnp.where(at, value[pl.ds(r, 1), :], 0.0).astype(BF)
        return 0

    lax.fori_loop(0, lats, spread_rows, 0)
    half = lats * width
    terms = dot_nt(spread[:, :half], marks[:, :half])
    value_pair.wait()
    value[pl.ds(lats, lats)] = value_in[...].astype(F32)
    lax.fori_loop(lats, 2 * lats, spread_rows, 0)
    terms = terms + dot_nt(spread[:, half:], marks[:, half:])
    terms_out[...] = terms.astype(BF).reshape(terms_out.shape)

    def terms_copy(k):
        return copy(
            terms_out.at[target(k)],
            terms_in.at[k],
            terms_send.at[k],
            terms_recv.at[k],
            sec=target(k) * 2 + core,
        )

    def terms_start(k, _):
        terms_copy(k).start()
        return 0

    lax.fori_loop(0, chips - 1, terms_start, 0)
    save(0, moist_out).start()
    save(1, heat_out).start()
    terms_in[chips - 1] = terms_out[chip]

    for i in (11, 12):
        loads[i].wait()
    groups = reaches // 128

    even = send_index[pl.ds(0, chips, stride=2), :]
    odd = send_index[pl.ds(1, chips, stride=2), :]
    flip = ones_where(iota((128, 128), 0) + iota((128, 128), 1) == 127)

    def halves(x):
        return jnp.concatenate([x // 128, x % 128], axis=0).astype(F32)

    pick_even = ones_where(
        iota((2 * chips, 2 * chips), 1) == 2 * (iota((2 * chips, 2 * chips), 0) % chips)
    )
    counts = dot_nt(
        pick_even, jnp.broadcast_to(send_count[...], (8, 2 * chips)).astype(F32).astype(BF)
    )
    pick_rows[pl.ds(0, 2 * chips)] = jnp.where(
        iota((2 * chips, cap), 1).astype(F32) < counts[:, 0:1],
        halves(even),
        dot(halves(odd).astype(BF), flip),
    )
    pick_rows[pl.ds(2 * chips, cap - 2 * chips)] = jnp.zeros((cap - 2 * chips, cap), F32)
    picks[...] = pick_rows[...].T
    loads[7].wait()
    loads[8].wait()
    lane_s = iota((cap, steps), 1)
    batch = pick.shape[0] // cap

    def pack(i, _):
        for b in range(batch):
            m = target(i * batch + b)
            at = column(picks[...], m) * 128.0 + column(picks[...], chips + m)
            pick[pl.ds(b * cap, cap), :] = ones_where(at.astype(I32) == iota((cap, reaches), 1))
        now = pl.ds(i * batch, batch)
        hydro_at[now] = dot(pick[...], hydro[...]).reshape(batch, cap, steps)
        moved = dot(pick[...], records[...])
        for b in range(batch):
            one = pltpu.roll(moved[b * cap : (b + 1) * cap], steps - 1, 1)
            shifted[i * batch + b] = jnp.where(lane_s == steps - 1, 0.0, one)
        return 0

    pack(0, 0)

    def terms_wait(k, _):
        terms_copy(k).wait()
        return 0

    lax.fori_loop(0, chips - 1, terms_wait, 0)
    reach_runoff = terms_in[0].astype(F32)
    for k in range(1, chips):
        reach_runoff = reach_runoff + terms_in[k].astype(F32)
    coarse = reach_runoff.astype(BF)
    fine = (reach_runoff - coarse.astype(F32)).astype(BF)
    both = jnp.concatenate([coarse.astype(F32), fine.astype(F32)], axis=0).astype(BF)
    parts = both.shape[0]

    def make_rows(k):
        m = target(k)
        index = column(picks[...], m) * 128.0 + column(picks[...], chips + m)
        octet = index.astype(I32) // 256
        found = dot(ones_where(octet == iota((cap, parts), 1) % (parts // 2)), both)
        at = index.astype(I32) % 256 == iota((cap, 256), 1)
        scale = jnp.sum(jnp.where(at, found, 0.0), axis=1, keepdims=True)
        return (shifted[k] + scale * hydro_at[k]).astype(BF)

    def rows_copy(k):
        return copy(
            rows_out.at[k],
            rows_in.at[k],
            rows_send.at[k],
            rows_recv.at[k],
            sec=target(k) * 2 + core,
        )

    def rows_start(k, _):
        rows_out[k] = make_rows(k)
        rows_copy(k).start()
        return 0

    lax.fori_loop(0, batch, rows_start, 0)

    for i in (9, 10):
        loads[i].wait()
    home = (homes[...] % (2 * inflow.shape[0])).astype(F32).T.astype(I32)
    table = jnp.concatenate([home // 256, home % 256], axis=0).astype(F32).astype(BF)
    def look(m, _):
        basin = basins[pl.ds(m, 1), :]
        found = dot(table, ones_where(basin // 128 == iota((128, 128), 0)))
        at = basin % 128 == iota((128, 128), 0)
        high = jnp.sum(jnp.where(at, found[:128], 0.0), axis=0, keepdims=True)
        low = jnp.sum(jnp.where(at, found[128:], 0.0), axis=0, keepdims=True)
        places[pl.ds(m, 1), :] = high
        places[pl.ds(groups + m, 1), :] = low
        return 0

    lax.fori_loop(0, groups, look, 0)

    place_cols = places[...].T.astype(BF)

    def ids_fill(m, _):
        group = pick_rows[pl.ds(m, 1), :].astype(I32)
        at = pick_rows[pl.ds(chips + m, 1), :].astype(I32) == iota((128, cap), 0)
        digit = iota((2 * groups, cap), 0)
        found = dot(
            place_cols,
            jnp.concatenate(
                [ones_where(digit == group), ones_where(digit == group + groups)], axis=1
            ),
        )
        high = jnp.sum(jnp.where(at, found[:, :cap], 0.0), axis=0, keepdims=True)
        low = jnp.sum(jnp.where(at, found[:, cap:], 0.0), axis=0, keepdims=True)
        ids_out[m] = (high * 256.0 + low).astype(I32)
        return 0

    lax.fori_loop(0, chips, ids_fill, 0)

    def ids_copy(k):
        return copy(
            ids_out.at[target(k)],
            ids_in.at[k],
            ids_send.at[k],
            ids_recv.at[k],
            sec=target(k) * 2 + core,
        )

    def ids_start(k, _):
        ids_copy(k).start()
        return 0

    lax.fori_loop(0, chips - 1, ids_start, 0)
    ids_in[chips - 1] = ids_out[chip]

    def more(i, _):
        pack(i, 0)
        lax.fori_loop(i * batch, jnp.minimum((i + 1) * batch, chips - 1), rows_start, 0)
        return 0

    lax.fori_loop(1, chips // batch, more, 0)
    rows_in[chips - 1] = make_rows(chips - 1)

    diagonal = iota((256, 256), 0) == iota((256, 256), 1)
    lane_w = iota((256, steps), 1)
    for j in range(reaches // 256):
        scale = jnp.sum(
            jnp.where(diagonal, reach_runoff[j : j + 1, :], 0.0), axis=1, keepdims=True
        )
        rows = pl.ds(j * 256, 256)
        moved = pltpu.roll(records[rows, :].astype(F32), steps - 1, 1)
        moved = jnp.where(lane_w == steps - 1, 0.0, moved)
        record_out[rows, :] = (moved + scale * hydro[rows, :].astype(F32)).astype(BF)

    save(2, record_out).start()
    def ids_wait(k, _):
        ids_copy(k).wait()
        return 0

    lax.fori_loop(0, chips - 1, ids_wait, 0)
    ids_pair = copy(ids_in, ids_near, pair_send.at[2], pair_recv.at[2], sec=partner)
    ids_pair.start()

    ids_pair.wait()
    mine = inflow.shape[0]
    basin_at = iota((mine, 2 * cap), 0) + core * mine

    def choose(i, _):
        for marked, ids in ((chosen, ids_in), (chosen_near, ids_near)):
            got = jnp.concatenate([ids[2 * i], ids[2 * i + 1]], axis=1)
            marked[i] = ones_where(got == basin_at)
        return 0

    lax.fori_loop(0, chips // 2, choose, 0)

    def gain(i, marked, rows):
        return dot(marked[i], rows[pl.ds(2 * i, 2)].reshape(2 * cap, steps))

    def near_copy(i):
        pair = pl.ds(2 * i, 2)
        return copy(
            rows_in.at[pair], rows_near.at[pair], near_send.at[i], near_recv.at[i], sec=partner
        )

    last = chips // 2 - 1
    rows_copy(0).wait()
    rows_copy(1).wait()
    near_copy(0).start()
    inflow[...] = gain(0, chosen, rows_in)

    def add(i, _):
        rows_copy(2 * i).wait()
        rows_copy(2 * i + 1).wait()
        near_copy(i).start()
        near_copy(i - 1).wait()
        inflow[...] += gain(i, chosen, rows_in) + gain(i - 1, chosen_near, rows_near)
        return 0

    lax.fori_loop(1, last, add, 0)
    rows_copy(chips - 2).wait()
    near_copy(last).start()
    near_copy(last - 1).wait()
    inflow[...] += gain(last, chosen, rows_in) + gain(last - 1, chosen_near, rows_near)
    near_copy(last).wait()
    inflow[...] += gain(last, chosen_near, rows_near)
    save(3, inflow).start()
    for i, done in enumerate((moist_out, heat_out, record_out, inflow)):
        save(i, done).wait()


def hand_over(*refs):
    srcs, dsts, held, load_sem, save_sem = refs[:4], refs[4:8], refs[8:12], refs[12], refs[13]
    order = (2, 3, 0, 1)
    loads = [pltpu.make_async_copy(srcs[i], held[i], load_sem.at[i]) for i in range(4)]
    saves = [pltpu.make_async_copy(held[i], dsts[i], save_sem.at[i]) for i in range(4)]
    for i in order:
        loads[i].start()
    for i in order:
        loads[i].wait()
        saves[i].start()
    for i in order:
        saves[i].wait()


def per_device(
    moisture,
    heat,
    moist_cond,
    heat_cond,
    rain,
    surface_flux,
    cell_reach,
    records,
    unit_hydro,
    down_basin,
    basin_home,
    send_index,
    send_count,
):
    sections = lax.axis_size("sec")
    chips = sections // 2
    layers, lats, width = moisture.shape
    reaches, steps = records.shape[1:]
    cap = send_index.shape[3]
    mine = basin_home.shape[1] // sections
    field = (2, layers, lats, width)
    octets = reaches // 256
    vmem = pltpu.VMEM
    sem = pltpu.SemaphoreType.DMA
    args = (
        moisture,
        heat,
        moist_cond,
        heat_cond,
        rain,
        surface_flux,
        cell_reach,
        records[0],
        unit_hydro[0],
        down_basin.reshape(reaches // 128, 128),
        basin_home.reshape(-1, 128),
        send_index[0, 0],
        send_count[0],
    )
    results = (
        jax.ShapeDtypeStruct((layers * lats, width), F32),
        jax.ShapeDtypeStruct((layers * lats, width), F32),
        jax.ShapeDtypeStruct((reaches, steps), BF),
        jax.ShapeDtypeStruct((mine, steps), F32),
    )
    anywhere = pl.BlockSpec(memory_space=pl.ANY)
    out = pl.pallas_call(
        kernel,
        out_shape=results,
        in_specs=[anywhere] * 13,
        out_specs=(anywhere,) * 4,
        scratch_shapes=[vmem(a.shape, a.dtype) for a in args + results]
        + [
            vmem(field, F32),
            vmem(field, F32),
            vmem(field, F32),
            vmem(field, F32),
            vmem((2, 2, layers, width), BF),
            vmem((2, 2, layers, width), BF),
            vmem((2, lats, 128), F32),
            vmem((2, lats, 128), F32),
            vmem((lats, width), I32),
            vmem((lats, width), BF),
            vmem((lats, width), BF),
            vmem((2 * lats, width), I32),
            vmem((2 * lats, width), I32),
            vmem((2 * lats, width), F32),
            vmem((chips * octets, 2 * lats * width), BF),
            vmem((256, 2 * lats * width), BF),
            vmem((chips, octets, 256), BF),
            vmem((chips, octets, 256), BF),
            vmem((2 * reaches // 128, 128), F32),
            vmem((cap, cap), F32),
            vmem((cap, cap), F32),
            vmem((chips, 1, cap), I32),
            vmem((chips, 1, cap), I32),
            vmem((chips, 1, cap), I32),
            vmem((4 * cap, reaches), BF),
            vmem((chips, cap, steps), F32),
            vmem((chips, cap, steps), F32),
            vmem((chips, cap, steps), BF),
            vmem((chips, cap, steps), BF),
            vmem((chips, cap, steps), BF),
            vmem((chips // 2, mine, 2 * cap), BF),
            vmem((chips // 2, mine, 2 * cap), BF),
            sem((13,)),
            sem((4,)),
            sem((4,)),
            sem((4,)),
            sem((3,)),
            sem((3,)),
            sem((chips,)),
            sem((chips,)),
            sem((chips,)),
            sem((chips,)),
            sem((chips,)),
            sem((chips,)),
            sem((chips // 2,)),
            sem((chips // 2,)),
        ],
        compiler_params=pltpu.CompilerParams(
            collective_id=0, has_side_effects=True, vmem_limit_bytes=60 * 1024 * 1024
        ),
    )(*args)
    out = pl.pallas_call(
        hand_over,
        out_shape=results,
        in_specs=[anywhere] * 4,
        out_specs=(anywhere,) * 4,
        scratch_shapes=[vmem(a.shape, a.dtype) for a in results] + [sem((4,)), sem((4,))],
    )(*out)
    fields = (layers, lats, width)
    return out[0].reshape(fields), out[1].reshape(fields), out[2][None], out[3][None]


def solution(mesh):
    placed = (
        P(None, "sec", "lon"),
        P(None, "sec", "lon"),
        P(None, "sec", "lon"),
        P(None, "sec", "lon"),
        P("sec", "lon"),
        P("sec", "lon"),
        P("sec", "lon"),
        P("lon", "sec", None),
        P("lon", "sec", None),
        P("lon", "sec"),
        P("lon", None),
        P("lon", "sec", None, None),
        P("lon", "sec", None),
    )
    return jax.shard_map(
        per_device,
        mesh=mesh,
        in_specs=placed,
        out_specs=(
            P(None, "sec", "lon"),
            P(None, "sec", "lon"),
            P("lon", "sec", None),
            P("lon", "sec", None),
        ),
        check_vma=False,
    )
```

```python
import jax
import jax.numpy as jnp
from jax import lax
from jax.experimental import pallas as pl
from jax.experimental.pallas import tpu as pltpu
from jax.sharding import PartitionSpec as P

LATERAL = 0.2
BF = jnp.bfloat16
F32 = jnp.float32
I32 = jnp.int32
NT = (((1,), (1,)), ((), ()))


def iota(shape, axis):
    return lax.broadcasted_iota(I32, shape, axis)


def ones_where(mask):
    return jnp.where(mask, 1.0, 0.0).astype(BF)


def dot(a, b):
    return jnp.dot(a, b, preferred_element_type=F32)


def dot_nt(a, b):
    return lax.dot_general(a, b, NT, preferred_element_type=F32)


def column(block, lane):
    shape = block.shape
    return jnp.sum(jnp.where(iota(shape, 1) == lane, block, 0.0), axis=1, keepdims=True)


def kernel(*refs):
    hbm, outs, rest = refs[:13], refs[13:17], refs[17:]
    local, rest = rest[:13], rest[13:]
    moist_out, heat_out, record_out, inflow, rest = *rest[:4], rest[4:]
    moist, heat, moist_cond, heat_cond, rain, flux, cells = local[:7]
    records, hydro, basins, homes, send_index, send_count = local[7:]
    (
        base,
        inv,
        back,
        ratio,
        row_out,
        row_in,
        col_out,
        col_in,
        cells_in,
        value_out,
        value_in,
        hi,
        lo,
        value,
        spread,
        marks,
        terms_out,
        terms_in,
        places,
        pick_rows,
        picks,
        ids_out,
        ids_in,
        ids_near,
        pick,
        shifted,
        hydro_at,
        rows_out,
        rows_in,
        rows_near,
        chosen,
        chosen_near,
        load_sem,
        save_sem,
        halo_send,
        halo_recv,
        pair_send,
        pair_recv,
        terms_send,
        terms_recv,
        ids_send,
        ids_recv,
        rows_send,
        rows_recv,
        near_send,
        near_recv,
    ) = rest
    layers, lats, width = moist.shape
    chips = rows_out.shape[0]
    cap = rows_out.shape[1]
    steps = rows_out.shape[2]
    reaches = records.shape[0]
    lon, sec = lax.axis_index("lon"), lax.axis_index("sec")
    n_lon, n_sec = lax.axis_size("lon"), lax.axis_size("sec")
    chip, core = sec // 2, sec % 2
    partner = chip * 2 + 1 - core
    up, down = (sec + n_sec - 1) % n_sec, (sec + 1) % n_sec
    left, right = (lon + n_lon - 1) % n_lon, (lon + 1) % n_lon

    def ahead(k):
        return chips // 2 + ((k + 1) // 2) * (2 * (k % 2) - 1)

    def target(k):
        return (chip + ahead(k)) % chips

    def copy(src, dst, send, recv, **where):
        return pltpu.make_async_remote_copy(
            src_ref=src, dst_ref=dst, send_sem=send, recv_sem=recv, device_id=where
        )

    barrier = pltpu.get_barrier_semaphore()

    def greet(k, _):
        pl.semaphore_signal(barrier, inc=1, device_id={"sec": target(k) * 2 + core})
        return 0

    lax.fori_loop(0, chips - 1, greet, 0)
    for peer in ({"sec": up}, {"sec": down}, {"lon": left}, {"lon": right}):
        pl.semaphore_signal(barrier, inc=1, device_id=peer)

    loads = [
        pltpu.make_async_copy(src, dst, load_sem.at[i])
        for i, (src, dst) in enumerate(zip(hbm, local))
    ]
    for i in (0, 1, 2, 3, 4, 5, 6, 9, 10, 11, 12, 7, 8):
        loads[i].start()

    def save(i, src):
        return pltpu.make_async_copy(src, outs[i], save_sem.at[i])

    for i in range(2):
        loads[i].wait()

    lane_e = iota((lats, 128), 1)
    first = jnp.zeros((lats, 128), F32)
    last = jnp.zeros((lats, 128), F32)
    for f, field in enumerate((moist, heat)):
        row_out[0, f] = field[:, 0, :].astype(BF)
        row_out[1, f] = field[:, lats - 1, :].astype(BF)
        for layer in range(layers):
            first = jnp.where(lane_e == f * layers + layer, field[layer, :, 0:1], first)
            last = jnp.where(
                lane_e == f * layers + layer, field[layer, :, width - 1 : width], last
            )
    col_out[0] = first
    col_out[1] = last

    for i in range(2, 7):
        loads[i].wait()
    row_at, lane_at = iota((lats, width), 0), iota((lats, width), 1)
    for f, (field, cond, extra) in enumerate(
        ((moist, moist_cond, rain), (heat, heat_cond, flux))
    ):
        for layer in range(layers):
            x = field[layer]
            near = (
                jnp.where(row_at == 0, 0.0, pltpu.roll(x, 1, 0))
                + jnp.where(row_at == lats - 1, 0.0, pltpu.roll(x, lats - 1, 0))
                + jnp.where(lane_at == 0, 0.0, pltpu.roll(x, 1, 1))
                + jnp.where(lane_at == width - 1, 0.0, pltpu.roll(x, width - 1, 1))
            )
            x = x + LATERAL * (near - 4.0 * x)
            base[f, layer] = x + extra[...] if layer == 0 else x
        prev = jnp.zeros((lats, width), F32)
        below = jnp.zeros((lats, width), F32)
        for layer in range(layers):
            if layer + 1 < layers:
                above = 0.5 * (cond[layer] + cond[layer + 1])
            else:
                above = jnp.zeros((lats, width), F32)
            part = 1.0 / (1.0 + below + above + below * prev)
            prev = -above * part
            inv[f, layer] = part
            back[f, layer] = below * part
            ratio[f, layer] = prev
            below = above

    def cell_marks(at, where):
        reach = where[...]
        rows = pl.ds(at, lats)
        hi[rows] = jnp.where(
            (reach // reaches) % 2 == core,
            (reach // (2 * reaches)) * (reaches // 256) + (reach // 256) % (reaches // 256),
            -1,
        )
        lo[rows] = reach % 256

        def mark(r, _):
            lanes = pl.ds(pl.multiple_of(r * width, width), width)
            marks[:, lanes] = ones_where(lo[pl.ds(r, 1), :] == iota((256, width), 0))
            return 0

        lax.fori_loop(at, at + lats, mark, 0)

    pl.semaphore_wait(barrier, chips - 1 + 4)

    halo = [
        copy(row_out.at[0], row_in.at[1], halo_send.at[0], halo_recv.at[1], sec=up),
        copy(row_out.at[1], row_in.at[0], halo_send.at[1], halo_recv.at[0], sec=down),
        copy(col_out.at[0], col_in.at[1], halo_send.at[2], halo_recv.at[3], lon=left),
        copy(col_out.at[1], col_in.at[0], halo_send.at[3], halo_recv.at[2], lon=right),
    ]
    reach_pair = copy(cells, cells_in, pair_send.at[0], pair_recv.at[0], sec=partner)
    for one in halo:
        one.start()
    reach_pair.start()
    cell_marks(0, cells)
    reach_pair.wait()
    cell_marks(lats, cells_in)
    for one in halo:
        one.wait()

    has_up = jnp.where(sec > 0, LATERAL, 0.0)
    has_down = jnp.where(sec < n_sec - 1, LATERAL, 0.0)
    has_left = jnp.where(lon > 0, LATERAL, 0.0)
    has_right = jnp.where(lon < n_lon - 1, LATERAL, 0.0)
    runoff = None
    surface = []
    for f, out in enumerate((moist_out, heat_out)):
        above_rows = row_in[0, f].astype(F32) * has_up
        below_rows = row_in[1, f].astype(F32) * has_down
        first = col_in[0] * has_left
        last = col_in[1] * has_right
        held = []
        prev = jnp.zeros((lats, width), F32)
        for layer in range(layers):
            lane = f * layers + layer
            source = (
                base[f, layer]
                + jnp.where(row_at == 0, above_rows[layer : layer + 1, :], 0.0)
                + jnp.where(row_at == lats - 1, below_rows[layer : layer + 1, :], 0.0)
                + jnp.where(lane_at == 0, first[:, lane : lane + 1], 0.0)
                + jnp.where(lane_at == width - 1, last[:, lane : lane + 1], 0.0)
            )
            prev = source * inv[f, layer] + back[f, layer] * prev
            held.append(prev)
        x = held[-1]
        out[pl.ds((layers - 1) * lats, lats), :] = x
        if f == 0:
            runoff = 0.5 * moist_cond[layers - 1] * x
        for layer in range(layers - 2, -1, -1):
            x = held[layer] - ratio[f, layer] * x
            out[pl.ds(layer * lats, lats), :] = x
        surface.append(x)
    wet = surface[0] - 1.0
    softplus = jnp.maximum(wet, 0.0) + jnp.log1p(jnp.exp(-jnp.abs(wet)))
    runoff = softplus * jax.nn.sigmoid(surface[1]) + runoff
    value_out[...] = runoff.astype(BF)
    value_pair = copy(value_out, value_in, pair_send.at[1], pair_recv.at[1], sec=partner)
    value_pair.start()
    value[pl.ds(0, lats)] = runoff

    def spread_rows(r, _):
        lanes = pl.ds(pl.multiple_of(r * width, width), width)
        at = hi[pl.ds(r, 1), :] == iota((spread.shape[0], width), 0)
        spread[:, lanes] = jnp.where(at, value[pl.ds(r, 1), :], 0.0).astype(BF)
        return 0

    lax.fori_loop(0, lats, spread_rows, 0)
    half = lats * width
    terms = dot_nt(spread[:, :half], marks[:, :half])
    value_pair.wait()
    value[pl.ds(lats, lats)] = value_in[...].astype(F32)
    lax.fori_loop(lats, 2 * lats, spread_rows, 0)
    terms = terms + dot_nt(spread[:, half:], marks[:, half:])
    terms_out[...] = terms.astype(BF).reshape(terms_out.shape)

    def terms_copy(k):
        return copy(
            terms_out.at[target(k)],
            terms_in.at[k],
            terms_send.at[k],
            terms_recv.at[k],
            sec=target(k) * 2 + core,
        )

    def terms_start(k, _):
        terms_copy(k).start()
        return 0

    lax.fori_loop(0, chips - 1, terms_start, 0)
    save(0, moist_out).start()
    save(1, heat_out).start()
    terms_in[chips - 1] = terms_out[chip]

    for i in (11, 12):
        loads[i].wait()
    groups = reaches // 128

    even = send_index[pl.ds(0, chips, stride=2), :]
    odd = send_index[pl.ds(1, chips, stride=2), :]
    flip = ones_where(iota((128, 128), 0) + iota((128, 128), 1) == 127)

    def halves(x):
        return jnp.concatenate([x // 128, x % 128], axis=0).astype(F32)

    pick_even = ones_where(
        iota((2 * chips, 2 * chips), 1) == 2 * (iota((2 * chips, 2 * chips), 0) % chips)
    )
    counts = dot_nt(
        pick_even, jnp.broadcast_to(send_count[...], (8, 2 * chips)).astype(F32).astype(BF)
    )
    pick_rows[pl.ds(0, 2 * chips)] = jnp.where(
        iota((2 * chips, cap), 1).astype(F32) < counts[:, 0:1],
        halves(even),
        dot(halves(odd).astype(BF), flip),
    )
    pick_rows[pl.ds(2 * chips, cap - 2 * chips)] = jnp.zeros((cap - 2 * chips, cap), F32)
    picks[...] = pick_rows[...].T
    loads[7].wait()
    loads[8].wait()
    lane_s = iota((cap, steps), 1)
    batch = pick.shape[0] // cap

    def pack(i, _):
        for b in range(batch):
            m = target(i * batch + b)
            at = column(picks[...], m) * 128.0 + column(picks[...], chips + m)
            pick[pl.ds(b * cap, cap), :] = ones_where(at.astype(I32) == iota((cap, reaches), 1))
        now = pl.ds(i * batch, batch)
        hydro_at[now] = dot(pick[...], hydro[...]).reshape(batch, cap, steps)
        moved = dot(pick[...], records[...])
        for b in range(batch):
            one = pltpu.roll(moved[b * cap : (b + 1) * cap], steps - 1, 1)
            shifted[i * batch + b] = jnp.where(lane_s == steps - 1, 0.0, one)
        return 0

    pack(0, 0)

    def terms_wait(k, _):
        terms_copy(k).wait()
        return 0

    lax.fori_loop(0, chips - 1, terms_wait, 0)
    reach_runoff = terms_in[0].astype(F32)
    for k in range(1, chips):
        reach_runoff = reach_runoff + terms_in[k].astype(F32)
    coarse = reach_runoff.astype(BF)
    fine = (reach_runoff - coarse.astype(F32)).astype(BF)
    both = jnp.concatenate([coarse.astype(F32), fine.astype(F32)], axis=0).astype(BF)
    parts = both.shape[0]

    def make_rows(k):
        m = target(k)
        index = column(picks[...], m) * 128.0 + column(picks[...], chips + m)
        octet = index.astype(I32) // 256
        found = dot(ones_where(octet == iota((cap, parts), 1) % (parts // 2)), both)
        at = index.astype(I32) % 256 == iota((cap, 256), 1)
        scale = jnp.sum(jnp.where(at, found, 0.0), axis=1, keepdims=True)
        return (shifted[k] + scale * hydro_at[k]).astype(BF)

    def rows_copy(k):
        return copy(
            rows_out.at[k],
            rows_in.at[k],
            rows_send.at[k],
            rows_recv.at[k],
            sec=target(k) * 2 + core,
        )

    def rows_start(k, _):
        rows_out[k] = make_rows(k)
        rows_copy(k).start()
        return 0

    lax.fori_loop(0, batch, rows_start, 0)

    for i in (9, 10):
        loads[i].wait()
    home = (homes[...] % (2 * inflow.shape[0])).astype(F32).T.astype(I32)
    table = jnp.concatenate([home // 256, home % 256], axis=0).astype(F32).astype(BF)
    def look(m, _):
        basin = basins[pl.ds(m, 1), :]
        found = dot(table, ones_where(basin // 128 == iota((128, 128), 0)))
        at = basin % 128 == iota((128, 128), 0)
        high = jnp.sum(jnp.where(at, found[:128], 0.0), axis=0, keepdims=True)
        low = jnp.sum(jnp.where(at, found[128:], 0.0), axis=0, keepdims=True)
        places[pl.ds(m, 1), :] = high
        places[pl.ds(groups + m, 1), :] = low
        return 0

    lax.fori_loop(0, groups, look, 0)

    place_cols = places[...].T.astype(BF)

    def ids_fill(m, _):
        group = pick_rows[pl.ds(m, 1), :].astype(I32)
        at = pick_rows[pl.ds(chips + m, 1), :].astype(I32) == iota((128, cap), 0)
        digit = iota((2 * groups, cap), 0)
        found = dot(
            place_cols,
            jnp.concatenate(
                [ones_where(digit == group), ones_where(digit == group + groups)], axis=1
            ),
        )
        high = jnp.sum(jnp.where(at, found[:, :cap], 0.0), axis=0, keepdims=True)
        low = jnp.sum(jnp.where(at, found[:, cap:], 0.0), axis=0, keepdims=True)
        ids_out[m] = (high * 256.0 + low).astype(I32)
        return 0

    lax.fori_loop(0, chips, ids_fill, 0)

    def ids_copy(k):
        return copy(
            ids_out.at[target(k)],
            ids_in.at[k],
            ids_send.at[k],
            ids_recv.at[k],
            sec=target(k) * 2 + core,
        )

    def ids_start(k, _):
        ids_copy(k).start()
        return 0

    lax.fori_loop(0, chips - 1, ids_start, 0)
    ids_in[chips - 1] = ids_out[chip]

    def more(i, _):
        pack(i, 0)
        lax.fori_loop(i * batch, jnp.minimum((i + 1) * batch, chips - 1), rows_start, 0)
        return 0

    lax.fori_loop(1, chips // batch, more, 0)
    rows_in[chips - 1] = make_rows(chips - 1)

    diagonal = iota((256, 256), 0) == iota((256, 256), 1)
    lane_w = iota((256, steps), 1)
    for j in range(reaches // 256):
        scale = jnp.sum(
            jnp.where(diagonal, reach_runoff[j : j + 1, :], 0.0), axis=1, keepdims=True
        )
        rows = pl.ds(j * 256, 256)
        moved = pltpu.roll(records[rows, :].astype(F32), steps - 1, 1)
        moved = jnp.where(lane_w == steps - 1, 0.0, moved)
        record_out[rows, :] = (moved + scale * hydro[rows, :].astype(F32)).astype(BF)

    save(2, record_out).start()
    def ids_wait(k, _):
        ids_copy(k).wait()
        return 0

    lax.fori_loop(0, chips - 1, ids_wait, 0)
    ids_pair = copy(ids_in, ids_near, pair_send.at[2], pair_recv.at[2], sec=partner)
    ids_pair.start()

    ids_pair.wait()
    mine = inflow.shape[0]
    basin_at = iota((mine, 2 * cap), 0) + core * mine

    def choose(i, _):
        for marked, ids in ((chosen, ids_in), (chosen_near, ids_near)):
            got = jnp.concatenate([ids[2 * i], ids[2 * i + 1]], axis=1)
            marked[i] = ones_where(got == basin_at)
        return 0

    lax.fori_loop(0, chips // 2, choose, 0)

    def gain(i, marked, rows):
        return dot(marked[i], rows[pl.ds(2 * i, 2)].reshape(2 * cap, steps))

    def near_copy(i):
        pair = pl.ds(2 * i, 2)
        return copy(
            rows_in.at[pair], rows_near.at[pair], near_send.at[i], near_recv.at[i], sec=partner
        )

    last = chips // 2 - 1

    def near_one(k, n):
        return copy(
            rows_in.at[k], rows_near.at[k], near_send.at[n], near_recv.at[n], sec=partner
        )

    own_near = near_one(chips - 1, last + 1)
    last_near = near_one(chips - 2, last)
    own_near.start()
    rows_copy(0).wait()
    rows_copy(1).wait()
    near_copy(0).start()
    inflow[...] = gain(0, chosen, rows_in)

    def add(i, _):
        rows_copy(2 * i).wait()
        rows_copy(2 * i + 1).wait()
        near_copy(i).start()
        near_copy(i - 1).wait()
        inflow[...] += gain(i, chosen, rows_in) + gain(i - 1, chosen_near, rows_near)
        return 0

    lax.fori_loop(1, last, add, 0)
    rows_copy(chips - 2).wait()
    last_near.start()
    near_copy(last - 1).wait()
    inflow[...] += gain(last, chosen, rows_in) + gain(last - 1, chosen_near, rows_near)
    own_near.wait()
    last_near.wait()
    inflow[...] += gain(last, chosen_near, rows_near)
    save(3, inflow).start()
    for i, done in enumerate((moist_out, heat_out, record_out, inflow)):
        save(i, done).wait()


def hand_over(*refs):
    srcs, dsts, held, load_sem, save_sem = refs[:4], refs[4:8], refs[8:12], refs[12], refs[13]
    loads, saves = [], []
    for i, parts in ((2, 4), (3, 2), (0, 1), (1, 1)):
        rows = held[i].shape[0] // parts
        for p in range(parts):
            at, n = pl.ds(p * rows, rows), len(loads)
            loads.append(
                pltpu.make_async_copy(srcs[i].at[at], held[i].at[at], load_sem.at[n])
            )
            saves.append(
                pltpu.make_async_copy(held[i].at[at], dsts[i].at[at], save_sem.at[n])
            )
    for one in loads:
        one.start()
    for load, save in zip(loads, saves):
        load.wait()
        save.start()
    for one in saves:
        one.wait()


def per_device(
    moisture,
    heat,
    moist_cond,
    heat_cond,
    rain,
    surface_flux,
    cell_reach,
    records,
    unit_hydro,
    down_basin,
    basin_home,
    send_index,
    send_count,
):
    sections = lax.axis_size("sec")
    chips = sections // 2
    layers, lats, width = moisture.shape
    reaches, steps = records.shape[1:]
    cap = send_index.shape[3]
    mine = basin_home.shape[1] // sections
    field = (2, layers, lats, width)
    octets = reaches // 256
    vmem = pltpu.VMEM
    sem = pltpu.SemaphoreType.DMA
    args = (
        moisture,
        heat,
        moist_cond,
        heat_cond,
        rain,
        surface_flux,
        cell_reach,
        records[0],
        unit_hydro[0],
        down_basin.reshape(reaches // 128, 128),
        basin_home.reshape(-1, 128),
        send_index[0, 0],
        send_count[0],
    )
    results = (
        jax.ShapeDtypeStruct((layers * lats, width), F32),
        jax.ShapeDtypeStruct((layers * lats, width), F32),
        jax.ShapeDtypeStruct((reaches, steps), BF),
        jax.ShapeDtypeStruct((mine, steps), F32),
    )
    anywhere = pl.BlockSpec(memory_space=pl.ANY)
    out = pl.pallas_call(
        kernel,
        out_shape=results,
        in_specs=[anywhere] * 13,
        out_specs=(anywhere,) * 4,
        scratch_shapes=[vmem(a.shape, a.dtype) for a in args + results]
        + [
            vmem(field, F32),
            vmem(field, F32),
            vmem(field, F32),
            vmem(field, F32),
            vmem((2, 2, layers, width), BF),
            vmem((2, 2, layers, width), BF),
            vmem((2, lats, 128), F32),
            vmem((2, lats, 128), F32),
            vmem((lats, width), I32),
            vmem((lats, width), BF),
            vmem((lats, width), BF),
            vmem((2 * lats, width), I32),
            vmem((2 * lats, width), I32),
            vmem((2 * lats, width), F32),
            vmem((chips * octets, 2 * lats * width), BF),
            vmem((256, 2 * lats * width), BF),
            vmem((chips, octets, 256), BF),
            vmem((chips, octets, 256), BF),
            vmem((2 * reaches // 128, 128), F32),
            vmem((cap, cap), F32),
            vmem((cap, cap), F32),
            vmem((chips, 1, cap), I32),
            vmem((chips, 1, cap), I32),
            vmem((chips, 1, cap), I32),
            vmem((4 * cap, reaches), BF),
            vmem((chips, cap, steps), F32),
            vmem((chips, cap, steps), F32),
            vmem((chips, cap, steps), BF),
            vmem((chips, cap, steps), BF),
            vmem((chips, cap, steps), BF),
            vmem((chips // 2, mine, 2 * cap), BF),
            vmem((chips // 2, mine, 2 * cap), BF),
            sem((13,)),
            sem((4,)),
            sem((4,)),
            sem((4,)),
            sem((3,)),
            sem((3,)),
            sem((chips,)),
            sem((chips,)),
            sem((chips,)),
            sem((chips,)),
            sem((chips,)),
            sem((chips,)),
            sem((chips // 2 + 1,)),
            sem((chips // 2 + 1,)),
        ],
        compiler_params=pltpu.CompilerParams(
            collective_id=0, has_side_effects=True, vmem_limit_bytes=60 * 1024 * 1024
        ),
    )(*args)
    out = pl.pallas_call(
        hand_over,
        out_shape=results,
        in_specs=[anywhere] * 4,
        out_specs=(anywhere,) * 4,
        scratch_shapes=[vmem(a.shape, a.dtype) for a in results] + [sem((8,)), sem((8,))],
    )(*out)
    fields = (layers, lats, width)
    return out[0].reshape(fields), out[1].reshape(fields), out[2][None], out[3][None]


def solution(mesh):
    placed = (
        P(None, "sec", "lon"),
        P(None, "sec", "lon"),
        P(None, "sec", "lon"),
        P(None, "sec", "lon"),
        P("sec", "lon"),
        P("sec", "lon"),
        P("sec", "lon"),
        P("lon", "sec", None),
        P("lon", "sec", None),
        P("lon", "sec"),
        P("lon", None),
        P("lon", "sec", None, None),
        P("lon", "sec", None),
    )
    return jax.shard_map(
        per_device,
        mesh=mesh,
        in_specs=placed,
        out_specs=(
            P(None, "sec", "lon"),
            P(None, "sec", "lon"),
            P("lon", "sec", None),
            P("lon", "sec", None),
        ),
        check_vma=False,
    )
```
